512 devices in a mesh: chan: 4 (over x), pair: 128 (over y, z, core).
Axes of the slice: x: 4, y: 8, z: 8, core: 2. Of those that a mesh axis runs over, the one named last changes fastest.
Arguments:
- visibility: bfloat16 [4, 65536, 256], P('chan', 'pair'), may hold values from -6 to 6
- pair_counts: int32 [65536], P('pair'), may hold values from 1 to 4
- owner_ids: int32 [65536, 1], P('pair'), may hold values from 0 to 127; in each aligned block of 512 rows (0 to 511, 512 to 1023, ...) at most 12 rows name the same one
- slot_ids: int32 [65536], P('pair'), may hold values from 0 to 127
- beam: float32 [4, 2, 2, 16384, 1024], P('chan', None, None, 'pair'), may hold values from -0.125 to 0.125
Outputs:
- modes: float32 [4, 1024, 2, 2, 64], P('chan', 'pair')
- mode_power: float32 [1024, 2], P('pair')
The draws below stay inside these ranges and needn't reach their ends.
Inputs may be any that keep to these rules, and one draw needn't show every extreme that they name: `owner_ids`: among the 512 feed pairs of one device, no owner is named more than 12 times, a bound that some block reaches.
All inputs are finite; a program needn't handle non-finite values.
Results may differ from the reference program's by a relative error of at most 0.0017.
Values may be sent and summed in bfloat16 or wider, within the bound.
A program may use at most 64 MiB of HBM per device.

```python
import math
import jax
import jax.numpy as jnp
import numpy as np
from jax import lax

CHAN = 4
PAIR_DEV = 512
PAIRS = 65536
BASE = 16384
BASE_DEV = 128
MODES = 1024
MWIN = 2
SETS = 64
COLS = 256
CAP = 12
N_PAIR = 128


def touch_ends(values, own_key, smallest, top_value):
    spot = [jax.random.randint(jax.random.fold_in(own_key, axis), (), 0, length) for axis, length in enumerate(values.shape)]
    longest = values.shape.index(max(values.shape))
    neighbour = spot[:longest] + [(spot[longest] + 1) % values.shape[longest]] + spot[longest + 1:]
    return values.at[tuple(spot)].set(smallest).at[tuple(neighbour)].set(top_value)


def raised(entries, own_key, source, target, blocks, factor):
    def block_of(position):
        return (jnp.arange(entries.shape[position]) // (entries.shape[position] // blocks)).reshape((-1,) + (1,) * (entries.ndim - 1 - position))

    one_side = jax.random.permutation(own_key, blocks)[block_of(target)]
    other_side = (block_of(target) + blocks // 2) % blocks
    return jnp.where((block_of(source) == one_side) | (block_of(source) == other_side), factor * entries, entries)


def shard_levels(stream_key, dims, cuts, low, high):
    level, own = 1.0, jax.random.fold_in(stream_key, 6)
    for dim, parts in cuts:
        draws = jnp.exp(jax.random.uniform(jax.random.fold_in(own, dim), (parts,), jnp.float32, low / len(cuts), high / len(cuts)))
        level = level * jnp.repeat(draws, dims[dim] // parts).reshape([-1 if axis == dim else 1 for axis in range(len(dims))])
    return level


def routed_block(stream_key, own, number, rows, number_of, top, bound, lean):
    ranking = jax.random.permutation(stream_key, number_of)
    heavy_load, ordinary = portions_of(number_of, rows * top, bound, lean, True), portions_of(number_of, rows * top, bound, lean, False)
    places = jnp.arange(number_of)

    def named(tallies, turn):
        used = int((tallies > 0).sum())
        fixed = max(1, used // 4)
        passed = fixed + (places - fixed + turn * (used - fixed)) % max(1, number_of - fixed)
        return jnp.zeros((number_of,), jnp.int32).at[ranking[jnp.where(places < fixed, places, passed)]].set(jnp.asarray(tallies, jnp.int32))

    tallies = jnp.where(number % 4 == 0, named(heavy_load, number // 4), named(ordinary, number - number // 4 - 1))
    mixed = jax.random.permutation(jax.random.fold_in(own, 3), number_of)
    giver, sink = mixed[0:number_of // 2 * 2:2], mixed[1:number_of // 2 * 2:2]
    room = jnp.minimum(tallies[giver] - 1, bound - tallies[sink]) // 2
    room = jnp.where((giver == ranking[0]) | (sink == ranking[0]) | (tallies[sink] == 0), 0, jnp.maximum(room, 0))
    passed = jax.random.randint(jax.random.fold_in(own, 4), (number_of // 2,), 0, 1 << 20) % (room + 1)
    tallies = tallies.at[giver].add(-passed).at[sink].add(passed)
    items = jnp.searchsorted(jnp.cumsum(tallies), jnp.arange(rows * top), side="right").astype(jnp.int32)
    table = items.reshape(top, rows).T
    table = table[jax.random.permutation(jax.random.fold_in(own, 1), rows)]
    turn = jax.random.randint(jax.random.fold_in(own, 2), (rows, 1), 0, top)
    return jnp.take_along_axis(table, (jnp.arange(top)[None, :] + turn) % top, axis=1)


def portions_of(count, total, limit, skew, full):
    portions = [(1 << 20) // math.isqrt(standing ** skew) + 1 for standing in range(1, count + 1)]
    largest = limit if full else min(limit, max(-(-total // count), total * portions[0] // sum(portions)))
    least = 1 if total - largest >= count - 1 else 0
    given, spare = [largest] + [least] * (count - 1), total - largest - least * (count - 1)
    while spare > 0:
        movable = [i for i in range(1, count) if given[i] < largest] or [i for i in range(1, count) if given[i] < limit]
        whole, left = sum([portions[i] for i in movable]), spare
        for i in movable:
            addition = min(limit - given[i], max(1, left * portions[i] // whole), spare)
            given[i] = given[i] + addition
            spare = spare - addition
    return np.array(given)


def centred(own_key, shape, scale, limit, cuts=(), held_as=jnp.bfloat16):
    values = jax.random.normal(own_key, shape, jnp.float32) * scale
    if len(cuts) > 0:
        values = shard_levels(own_key, shape, cuts, -0.22, 0.18) * values
    return jnp.clip(values, min=-limit, max=limit).astype(held_as)


def noise_with(key, dims, scale, bound, shards, heavy, held_as=jnp.bfloat16):
    values = scale * jax.random.normal(key, dims, jnp.float32)
    if shards:
        values = values * shard_levels(key, dims, shards, -0.22, 0.18)
    return jnp.clip(raised(values, jax.random.fold_in(key, 3), *heavy), -bound, bound).astype(held_as)


def setup_inputs(seed: int = 0) -> dict:
    streams_of = jax.random.split(jax.random.key(seed), 6)
    visibility = centred(streams_of[0], (CHAN, PAIRS, COLS), 1.0, 6.0, ((0, 4), (1, 128)))
    pair_counts = touch_ends(jax.random.randint(streams_of[1], (PAIRS,), 1, 5), jax.random.fold_in(streams_of[1], 1), 1, 4).astype(jnp.int32)
    owner_ids_keys = jax.random.split(jax.random.fold_in(streams_of[2], 1), PAIRS // PAIR_DEV)
    owner_ids_turns = jax.random.permutation(jax.random.fold_in(streams_of[2], 3), PAIRS // PAIR_DEV)
    owner_ids = jax.vmap(lambda own, number: routed_block(jax.random.fold_in(streams_of[2], 2), own, number, PAIR_DEV, N_PAIR, 1, CAP, 2))(owner_ids_keys, owner_ids_turns).reshape((PAIRS, 1))
    slot_ids = touch_ends(jax.random.randint(streams_of[3], (PAIRS,), 0, BASE_DEV), jax.random.fold_in(streams_of[3], 1), 0, BASE_DEV - 1).astype(jnp.int32)
    beam = noise_with(streams_of[4], (CHAN, MWIN, 2, BASE, MODES), (2 * BASE) ** -0.5, 0.125, ((0, 4), (3, 128)), (3, 4, 128, 5.5), jnp.float32)
    return {"visibility": visibility, "pair_counts": pair_counts, "owner_ids": owner_ids, "slot_ids": slot_ids, "beam": beam}


def project_channel(vis_chan, beam_chan, baseline, weight, denom):
    weighted = (vis_chan.astype(jnp.float32) * weight[:, None]).astype(jnp.bfloat16)
    numer = jax.ops.segment_sum(weighted.astype(jnp.float32), baseline, num_segments=BASE)
    stacked = numer / jnp.maximum(denom, 1.0)[:, None]
    stacked = stacked.reshape(BASE, MWIN, 2, SETS)
    outputs = []
    for m_index in range(MWIN):
        real_part = stacked[:, m_index, 0, :]
        imag_part = stacked[:, m_index, 1, :]
        first = jnp.concatenate([real_part, imag_part], axis=0)
        second = jnp.concatenate([imag_part, -real_part], axis=0)
        right = jnp.concatenate([first, second], axis=1)
        left = beam_chan[m_index].reshape(2 * BASE, MODES)
        result = lax.dot_general(left, right, (((0,), (0,)), ((), ())), precision=lax.Precision.HIGHEST, preferred_element_type=jnp.float32)
        outputs.append(result.reshape(MODES, 2, SETS))
    return jnp.stack(outputs, axis=1)


def reference(visibility, pair_counts, owner_ids, slot_ids, beam):
    baseline = (owner_ids[:, 0] * BASE_DEV + slot_ids).astype(jnp.int32)
    weight = pair_counts.astype(jnp.float32)
    denom = jax.ops.segment_sum(weight, baseline, num_segments=BASE)

    def one_channel(pieces):
        return project_channel(pieces[0], pieces[1], baseline, weight, denom)

    modes = lax.map(one_channel, (visibility, beam))
    mode_power = jnp.sum(modes * modes, axis=(0, 3, 4)) / (CHAN * SETS)
    return modes, mode_power
```

```python
import functools

import jax
import jax.numpy as jnp
from jax import lax
from jax.experimental import pallas as pl
from jax.experimental.pallas import tpu as pltpu
from jax.sharding import PartitionSpec as P

MESH = pl.DeviceIdType.MESH
F32, BF16, I32, I16 = jnp.float32, jnp.bfloat16, jnp.int32, jnp.int16


def iota(shape, axis):
    return lax.broadcasted_iota(I32, shape, axis)


def dot(a, b):
    return jnp.dot(a, b, preferred_element_type=F32)


def dot_nt(a, b):
    return lax.dot_general(a, b, (((1,), (1,)), ((), ())), preferred_element_type=F32)


def body(
    n, nchan, sets,
    owner_hbm, slot_hbm, count_hbm, vis_hbm, beam_hbm,
    modes_ref, power_ref,
    owner_ref, slot_ref, count_ref, vis_ref,
    send, recv, meta_send, meta_recv,
    beam_buf, beam_hi, beam_lo, hot_a, hot_b, inv_denom,
    part, core_recv, send2, recv2, scale_send, scale_recv, pow_send, pow_recv,
    in_sem, beam_sem, meta_s, meta_r, data_s, data_r, core_s, core_r, red_s, red_r, scale_s, scale_r, pow_s, pow_r,
):
    chan = lax.axis_index("chan")
    me = lax.axis_index("pair")
    chips = n // 2
    chip, core = me // 2, me % 2
    rows, columns = vis_ref.shape
    step_chips = min(8, chips)

    loads = [
        pltpu.make_async_copy(src, dst, in_sem.at[i])
        for i, (src, dst) in enumerate((
            (owner_hbm, owner_ref), (slot_hbm, slot_ref), (count_hbm, count_ref), (vis_hbm, vis_ref),
        ))
    ]
    for load in loads:
        load.start()
    beam_copy = pltpu.make_async_copy(beam_hbm, beam_buf, beam_sem)
    beam_copy.start()

    barrier = pltpu.get_barrier_semaphore()

    def greet(i, carry):
        peer = lax.rem(me + i, n)
        pl.semaphore_signal(barrier, inc=1, device_id={"chan": chan, "pair": peer}, device_id_type=MESH)
        return carry

    lax.fori_loop(1, n, greet, 0)
    for i in range(1, nchan):
        peer = lax.rem(chan + i, nchan)
        pl.semaphore_signal(barrier, inc=1, device_id={"chan": peer, "pair": me}, device_id_type=MESH)

    for load in loads:
        load.wait()

    owner = owner_ref[...]
    count = count_ref[...].astype(F32)
    slot = slot_ref[...].astype(F32)
    own_hot = jnp.where(iota((n, rows), 0) == owner, 1.0, 0.0).astype(BF16)
    before = jnp.where(iota((rows, rows), 0) < iota((rows, rows), 1), 1.0, 0.0).astype(BF16)
    rank = jnp.sum(own_hot.astype(F32) * dot(own_hot, before), axis=0, keepdims=True).astype(I32)

    lane_hit = iota((128, rows), 0) == rank
    by_slot = jnp.where(lane_hit, slot, 0.0).astype(BF16)
    by_count = jnp.where(lane_hit, count * 128.0, 0.0).astype(BF16)
    meta = dot_nt(own_hot, by_slot) + dot_nt(own_hot, by_count)
    meta_send[...] = meta.reshape(n, 1, 128)

    target_a = jnp.where(rank < 8, owner * 8 + rank, -1)
    target_b = jnp.where(rank >= 8, owner * 8 + rank - 8, -1)
    step_owners = min(16, n)
    step_rows = step_owners * 8

    def pack(i, carry):
        place = iota((step_rows, rows), 0) + i * step_rows
        pick_a = jnp.where(place == target_a, count, 0.0).astype(BF16)
        pick_b = jnp.where((place & -5) == target_b, count, 0.0).astype(BF16)
        vis = vis_ref[...]
        got_a = dot(pick_a, vis)
        got_b = dot(pick_b, vis)
        low = (iota((step_rows, 128), 0) & 4) == 0
        mixed = jnp.where(low, got_b[:, :128], got_b[:, 128:])
        at = pl.ds(i * step_owners, step_owners)
        send[at, 0] = got_a[:, :128].reshape(step_owners, 8, 128).astype(BF16)
        send[at, 1] = got_a[:, 128:].reshape(step_owners, 8, 128).astype(BF16)
        send[at, 2] = mixed.reshape(step_owners, 8, 128).astype(BF16)
        return carry

    lax.fori_loop(0, n // step_owners, pack, 0)

    pl.semaphore_wait(barrier, n - 1 + nchan - 1)

    own_meta = pltpu.make_async_copy(meta_send.at[me], meta_recv.at[me], meta_r)
    own_meta.start()
    own_data = pltpu.make_async_copy(send.at[me], recv.at[me], data_r)
    own_data.start()

    def send_meta(i, carry):
        peer = lax.rem(me + i, n)
        pltpu.make_async_remote_copy(
            meta_send.at[peer], meta_recv.at[me], meta_s, meta_r,
            device_id={"chan": chan, "pair": peer}, device_id_type=MESH).start()
        return carry

    lax.fori_loop(1, n, send_meta, 0)

    def send_data(i, carry):
        peer = lax.rem(me + i, n)
        pltpu.make_async_remote_copy(
            send.at[peer], recv.at[me], data_s, data_r,
            device_id={"chan": chan, "pair": peer}, device_id_type=MESH).start()
        return carry

    lax.fori_loop(1, n, send_data, 0)

    beam_copy.wait()
    mwin, modes = beam_buf.shape[0], beam_buf.shape[3]
    base = beam_buf.shape[2]
    for m in range(mwin):
        for r in range(2):
            def split(i, carry, m=m, r=r):
                at = pl.ds(i * 16, 16)
                full = beam_buf[m, r, at, :]
                high = full.astype(BF16)
                beam_hi[m, pl.ds(r * base + i * 16, 16), :] = high
                beam_lo[m, pl.ds(r * base + i * 16, 16), :] = (full - high.astype(F32)).astype(BF16)
                return carry

            lax.fori_loop(0, base // 16, split, 0)

    pltpu.make_async_copy(meta_recv, meta_recv, meta_r).wait()
    code = jnp.transpose(meta_recv[...].reshape(n, 128))[:16]
    weight = jnp.floor(code * (1.0 / 128.0))
    place = code - weight * 128.0
    both = jnp.concatenate([place, weight], axis=0).astype(BF16)
    spread = dot(both, jnp.where(iota((n, n * 8), 0) == iota((n, n * 8), 1) // 8, 1.0, 0.0).astype(BF16))
    ranks = iota((16, n * 8), 0)
    in_message = iota((16, n * 8), 1) & 7
    at_a = ranks == in_message
    at_b = ranks == 8 + (in_message & 3)

    def flat(values, mask):
        return jnp.sum(jnp.where(mask, values, 0.0), axis=0, keepdims=True)

    slot_a, slot_b = flat(spread[:16], at_a), flat(spread[:16], at_b)
    weight_a, weight_b = flat(spread[16:], at_a), flat(spread[16:], at_b)
    bases = iota((base, n * 8), 0).astype(F32)
    first = (iota((base, n * 8), 1) & 4) == 0
    hit_a = jnp.where(bases == slot_a, 1.0, 0.0)
    hit_b = jnp.where(bases == slot_b, 1.0, 0.0)
    hot_a[...] = hit_a.astype(BF16)
    hot_b[:base] = jnp.where(first, hit_b, 0.0).astype(BF16)
    hot_b[base:] = jnp.where(first, 0.0, hit_b).astype(BF16)
    denom = jnp.sum(hit_a * weight_a + jnp.where(first, hit_b, 0.0) * weight_b, axis=1, keepdims=True)
    inv_denom[...] = jnp.broadcast_to(jnp.maximum(denom, 1.0), (base, 128))

    pltpu.make_async_copy(recv, recv, data_r).wait()

    rows_0 = recv[:, 0].reshape(n * 8, 128)
    rows_1 = recv[:, 1].reshape(n * 8, 128)
    rows_2 = recv[:, 2].reshape(n * 8, 128)
    late = dot(hot_b[...], rows_2)
    numer = (dot(hot_a[...], rows_0) + late[:base], dot(hot_a[...], rows_1) + late[base:])
    sign = jnp.where(iota((base, 128), 1) < sets, 1.0, -1.0)
    for m in range(mwin):
        stacked = numer[m] / inv_denom[...]
        swapped = jnp.concatenate([stacked[:, sets:], stacked[:, :sets]], axis=1) * sign
        right = jnp.concatenate([jnp.transpose(stacked), jnp.transpose(swapped)], axis=1)
        high = right.astype(BF16)
        low = (right - high.astype(F32)).astype(BF16)
        step_modes = min(256, modes)

        def project(i, carry, m=m, high=high, low=low):
            at = pl.ds(pl.multiple_of(i * step_modes, step_modes), step_modes)
            hi = beam_hi[m, :, at]
            lo = beam_lo[m, :, at]
            sums = dot(high, hi) + (dot(low, hi) + dot(high, lo))
            blocks = jnp.transpose(sums).reshape(step_modes // 16, 2, 8, 128)
            part[pl.ds(i * (step_modes // 16), step_modes // 16), :, :, pl.ds(m * 128, 128)] = blocks
            return carry

        lax.fori_loop(0, modes // step_modes, project, 0)

    to_core = pltpu.make_async_remote_copy(
        part.at[:, 1 - core], core_recv, core_s, core_r,
        device_id={"chan": chan, "pair": me + 1 - 2 * core}, device_id_type=MESH)
    to_core.start()
    to_core.wait_recv()
    summed = part[:, core] + core_recv[...]
    core_recv[...] = summed
    peak = jnp.max(jnp.abs(summed), axis=(0, 1, 2), keepdims=True).reshape(1, 1)
    peak = jnp.maximum(peak, 1e-30)
    scale_send[...] = jnp.broadcast_to(peak * (1.0 / 32000.0), (1, 128))
    factor = jnp.broadcast_to(32000.0 / peak, (8, columns))

    def code_sums(i, carry):
        scaled = core_recv[pl.ds(i * step_chips, step_chips)] * factor
        send2[pl.ds(i * step_chips, step_chips)] = jnp.round(scaled).astype(I32).astype(I16)
        return carry

    lax.fori_loop(0, chips // step_chips, code_sums, 0)

    own_scale = pltpu.make_async_copy(scale_send, scale_recv.at[chip], scale_r)
    own_scale.start()
    own_red = pltpu.make_async_copy(send2.at[chip], recv2.at[chip], red_r)
    own_red.start()

    def send_red(i, carry):
        peer = lax.rem(chip + i, chips)
        pltpu.make_async_remote_copy(
            scale_send, scale_recv.at[chip], scale_s, scale_r,
            device_id={"chan": chan, "pair": peer * 2 + core}, device_id_type=MESH).start()
        pltpu.make_async_remote_copy(
            send2.at[peer], recv2.at[chip], red_s, red_r,
            device_id={"chan": chan, "pair": peer * 2 + core}, device_id_type=MESH).start()
        return carry

    lax.fori_loop(1, chips, send_red, 0)
    pltpu.make_async_copy(scale_recv, scale_recv, scale_r).wait()
    pltpu.make_async_copy(recv2, recv2, red_r).wait()

    def add_up(i, sums):
        scale = scale_recv[i]
        return sums + recv2[i].astype(I32).astype(F32) * jnp.concatenate([scale, scale], axis=1)

    total = lax.fori_loop(0, chips, add_up, jnp.zeros((8, columns), F32))
    modes_ref[...] = total
    square = total * total
    power_0 = jnp.sum(square[:, :128], axis=1, keepdims=True)
    power_1 = jnp.sum(square[:, 128:], axis=1, keepdims=True)
    pow_send[...] = jnp.where(iota((8, 128), 1) == 0, power_0, power_1)
    pow_recv[chan] = pow_send[...]
    sends = []
    for i in range(1, nchan):
        peer = lax.rem(chan + i, nchan)
        copy = pltpu.make_async_remote_copy(
            pow_send, pow_recv.at[chan], pow_s.at[i], pow_r.at[i],
            device_id={"chan": peer, "pair": me}, device_id_type=MESH)
        copy.start()
        sends.append(copy)
    for copy in sends:
        copy.wait()
    power = jnp.sum(pow_recv[...], axis=0) * (1.0 / (nchan * sets))
    power_ref[...] = power[:, :2]

    to_core.wait_send()
    pltpu.make_async_copy(meta_send.at[pl.ds(1, n - 1)], meta_send.at[pl.ds(1, n - 1)], meta_s).wait()
    pltpu.make_async_copy(send.at[pl.ds(1, n - 1)], send.at[pl.ds(1, n - 1)], data_s).wait()
    pltpu.make_async_copy(send2.at[pl.ds(1, chips - 1)], send2.at[pl.ds(1, chips - 1)], red_s).wait()
    pltpu.make_async_copy(scale_recv.at[pl.ds(1, chips - 1)], scale_recv.at[pl.ds(1, chips - 1)], scale_s).wait()


def per_device(visibility, pair_counts, owner_ids, slot_ids, beam):
    n, nchan = lax.axis_size("pair"), lax.axis_size("chan")
    rows, columns = visibility.shape[1:]
    mwin, _, base, modes = beam.shape[1:]
    sets = columns // (2 * mwin)
    chips = n // 2
    vmem, hbm = pl.BlockSpec(memory_space=pltpu.VMEM), pl.BlockSpec(memory_space=pl.ANY)
    dma = pltpu.SemaphoreType.DMA
    amplitudes, power = pl.pallas_call(
        functools.partial(body, n, nchan, sets),
        out_shape=(
            jax.ShapeDtypeStruct((8, columns), F32),
            jax.ShapeDtypeStruct((8, mwin), F32),
        ),
        in_specs=[hbm] * 5,
        out_specs=(vmem, vmem),
        scratch_shapes=[
            pltpu.VMEM((1, rows), I32),
            pltpu.VMEM((1, rows), I32),
            pltpu.VMEM((1, rows), I32),
            pltpu.VMEM((rows, columns), BF16),
            pltpu.VMEM((n, 3, 8, 128), BF16),
            pltpu.VMEM((n, 3, 8, 128), BF16),
            pltpu.VMEM((n, 1, 128), F32),
            pltpu.VMEM((n, 1, 128), F32),
            pltpu.VMEM((mwin, 2, base, modes), F32),
            pltpu.VMEM((mwin, 2 * base, modes), BF16),
            pltpu.VMEM((mwin, 2 * base, modes), BF16),
            pltpu.VMEM((base, n * 8), BF16),
            pltpu.VMEM((2 * base, n * 8), BF16),
            pltpu.VMEM((base, 128), F32),
            pltpu.VMEM((chips, 2, 8, columns), F32),
            pltpu.VMEM((chips, 8, columns), F32),
            pltpu.VMEM((chips, 8, columns), I16),
            pltpu.VMEM((chips, 8, columns), I16),
            pltpu.VMEM((1, 128), F32),
            pltpu.VMEM((chips, 1, 128), F32),
            pltpu.VMEM((8, 128), F32),
            pltpu.VMEM((nchan, 8, 128), F32),
            dma((4,)), dma, dma, dma, dma, dma, dma, dma, dma, dma, dma, dma,
            dma((nchan,)), dma((nchan,)),
        ],
        compiler_params=pltpu.CompilerParams(
            collective_id=0, has_side_effects=True
        ),
        name="stack_project",
    )(
        owner_ids.reshape(1, rows), slot_ids.reshape(1, rows), pair_counts.reshape(1, rows),
        visibility[0], beam[0],
    )
    return amplitudes.reshape(1, 8, mwin, 2, sets), power


def solution(mesh):
    in_specs = (
        P("chan", "pair", None),
        P("pair"),
        P("pair", None),
        P("pair"),
        P("chan", None, None, "pair", None),
    )
    out_specs = (P("chan", "pair", None, None, None), P("pair", None))
    return jax.shard_map(
        per_device, mesh=mesh, in_specs=in_specs, out_specs=out_specs, check_vma=False
    )
```

```python
import functools

import jax
import jax.numpy as jnp
from jax import lax
from jax.experimental import pallas as pl
from jax.experimental.pallas import tpu as pltpu
from jax.sharding import PartitionSpec as P

MESH = pl.DeviceIdType.MESH
F32, BF16, I32, I16 = jnp.float32, jnp.bfloat16, jnp.int32, jnp.int16


def iota(shape, axis):
    return lax.broadcasted_iota(I32, shape, axis)


def dot(a, b):
    return jnp.dot(a, b, preferred_element_type=F32)


def dot_nt(a, b):
    return lax.dot_general(a, b, (((1,), (1,)), ((), ())), preferred_element_type=F32)


def body(
    n, nchan, sets,
    owner_hbm, slot_hbm, count_hbm, vis_hbm, beam_hbm,
    modes_ref, power_ref,
    owner_ref, slot_ref, count_ref, vis_ref,
    send, recv, meta_send, meta_recv,
    beam_buf, beam_t, hot_a, hot_b, bottom, right,
    part, core_recv, send2, recv2, scale_send, scale_recv, pow_send, pow_recv,
    in_sem, beam_sem, meta_s, meta_r, data_s, data_r, core_s, core_r, red_s, red_r, scale_s, scale_r, pow_s, pow_r,
):
    chan = lax.axis_index("chan")
    me = lax.axis_index("pair")
    chips = n // 2
    chip, core = me // 2, me % 2
    rows, columns = vis_ref.shape
    step_chips = min(8, chips)

    loads = [
        pltpu.make_async_copy(src, dst, in_sem.at[i])
        for i, (src, dst) in enumerate((
            (owner_hbm, owner_ref), (slot_hbm, slot_ref), (count_hbm, count_ref), (vis_hbm, vis_ref),
        ))
    ]
    for load in loads:
        load.start()
    beam_copy = pltpu.make_async_copy(beam_hbm, beam_buf, beam_sem)
    beam_copy.start()

    barrier = pltpu.get_barrier_semaphore()

    side = 8
    while side * side > chips:
        side //= 2
    depth = chips // side
    chip_row, chip_spot = lax.div(chip, side), lax.rem(chip, side)

    def far(k, size):
        half = lax.div(k, 2) if not isinstance(k, int) else k // 2
        return size // 2 + half - (k - 2 * half) * (2 * half + 1)

    def each_chip(visit):
        along = [lax.rem(chip_spot + far(k, side), side) for k in range(side)]

        def ring(k, carry):
            first = lax.rem(chip_row + far(k, depth), depth) * side
            for step in along:
                visit(first + step)
            return carry

        lax.fori_loop(0, depth - 1, ring, 0)
        for step in along[:-1]:
            visit(chip_row * side + step)

    def greet(pair):
        pl.semaphore_signal(barrier, inc=1, device_id={"chan": chan, "pair": pair}, device_id_type=MESH)

    def greet_chip(peer):
        greet(peer * 2)
        greet(peer * 2 + 1)

    each_chip(greet_chip)
    greet(chip * 2 + 1 - core)
    for i in range(1, nchan):
        peer = lax.rem(chan + i, nchan)
        pl.semaphore_signal(barrier, inc=1, device_id={"chan": peer, "pair": me}, device_id_type=MESH)

    for load in loads:
        load.wait()

    owner = owner_ref[...]
    count = count_ref[...].astype(F32)
    slot = slot_ref[...].astype(F32)
    own_hot = jnp.where(iota((n, rows), 0) == owner, 1.0, 0.0).astype(BF16)
    before = jnp.where(iota((rows, rows), 0) < iota((rows, rows), 1), 1.0, 0.0).astype(BF16)
    rank = jnp.sum(own_hot.astype(F32) * dot(own_hot, before), axis=0, keepdims=True).astype(I32)

    lane_hit = iota((128, rows), 0) == rank
    by_slot = jnp.where(lane_hit, slot, 0.0).astype(BF16)
    by_count = jnp.where(lane_hit, count * 128.0, 0.0).astype(BF16)
    meta = dot_nt(own_hot, by_slot) + dot_nt(own_hot, by_count)
    meta_send[...] = meta.reshape(n, 1, 128)

    target_a = jnp.where(rank < 8, owner * 8 + rank, -1)
    target_b = jnp.where(rank >= 8, owner * 8 + rank - 8, -1)
    step_owners = min(16, n)
    step_rows = step_owners * 8

    def pack(i, carry):
        place = iota((step_rows, rows), 0) + i * step_rows
        pick_a = jnp.where(place == target_a, count, 0.0).astype(BF16)
        pick_b = jnp.where((place & -5) == target_b, count, 0.0).astype(BF16)
        vis = vis_ref[...]
        got_a = dot(pick_a, vis)
        got_b = dot(pick_b, vis)
        low = (iota((step_rows, 128), 0) & 4) == 0
        mixed = jnp.where(low, got_b[:, :128], got_b[:, 128:])
        at = pl.ds(i * step_owners, step_owners)
        send[at, 0] = got_a[:, :128].reshape(step_owners, 8, 128).astype(BF16)
        send[at, 1] = got_a[:, 128:].reshape(step_owners, 8, 128).astype(BF16)
        send[at, 2] = mixed.reshape(step_owners, 8, 128).astype(BF16)
        return carry

    lax.fori_loop(0, n // step_owners, pack, 0)

    pl.semaphore_wait(barrier, n - 1 + nchan - 1)

    own_meta = pltpu.make_async_copy(meta_send.at[me], meta_recv.at[me], meta_r)
    own_meta.start()
    own_data = pltpu.make_async_copy(send.at[me], recv.at[me], data_r)
    own_data.start()

    def ship(peer):
        target = {"chan": chan, "pair": peer}
        pltpu.make_async_remote_copy(
            meta_send.at[peer], meta_recv.at[me], meta_s, meta_r,
            device_id=target, device_id_type=MESH).start()
        pltpu.make_async_remote_copy(
            send.at[peer], recv.at[me], data_s, data_r,
            device_id=target, device_id_type=MESH).start()

    def ship_chip(peer):
        ship(peer * 2 + core)
        ship(peer * 2 + 1 - core)

    each_chip(ship_chip)
    ship(chip * 2 + 1 - core)

    beam_copy.wait()
    mwin, modes = beam_buf.shape[0], beam_buf.shape[3]
    base = beam_buf.shape[2]
    width = min(128, modes)
    turned = width // 2
    for m in range(mwin):
        for r in range(2):
            def turn(i, carry, m=m, r=r):
                at = pl.ds(pl.multiple_of(i * width, width), width)
                full = jnp.transpose(beam_buf[m, r, :, at])
                high = full.astype(BF16).astype(F32)
                low = full - high
                high, low = high.reshape(width // 16, 2, 8, base), low.reshape(width // 16, 2, 8, base)
                to = pl.ds(pl.multiple_of(i * turned, turned), turned)
                for half in range(2):
                    beam_t[m, half, to, r * base:(r + 1) * base] = high[:, half].reshape(turned, base).astype(BF16)
                    beam_t[m, half, to, (2 + r) * base:(3 + r) * base] = low[:, half].reshape(turned, base).astype(BF16)
                return carry

            lax.fori_loop(0, modes // width, turn, 0)

    right[:, 2 * base:, 128:] = jnp.zeros((mwin, 2 * base, 128), BF16)

    pltpu.make_async_copy(meta_recv, meta_recv, meta_r).wait()
    code = jnp.transpose(meta_recv[...].reshape(n, 128))[:16]
    weight = jnp.floor(code * (1.0 / 128.0))
    place = code - weight * 128.0
    both = jnp.concatenate([place, weight], axis=0).astype(BF16)
    spread = dot(both, jnp.where(iota((n, n * 8), 0) == iota((n, n * 8), 1) // 8, 1.0, 0.0).astype(BF16))
    ranks = iota((16, n * 8), 0)
    in_message = iota((16, n * 8), 1) & 7
    at_a = ranks == in_message
    at_b = ranks == 8 + (in_message & 3)

    def flat(values, mask):
        return jnp.sum(jnp.where(mask, values, 0.0), axis=0, keepdims=True)

    slot_a, slot_b = flat(spread[:16], at_a), flat(spread[:16], at_b)
    weight_a, weight_b = flat(spread[16:], at_a), flat(spread[16:], at_b)
    bases = iota((base, n * 8), 0).astype(F32)
    first = (iota((base, n * 8), 1) & 4) == 0
    hit_a = jnp.where(bases == slot_a, 1.0, 0.0)
    hit_b = jnp.where(bases == slot_b, 1.0, 0.0)
    hot_a[...] = hit_a.astype(BF16)
    hot_b[:base] = jnp.where(first, hit_b, 0.0).astype(BF16)
    hot_b[base:] = jnp.where(first, 0.0, hit_b).astype(BF16)
    denom = jnp.sum(hit_a * weight_a + jnp.where(first, hit_b, 0.0) * weight_b, axis=1, keepdims=True)
    bottom[...] = jnp.broadcast_to(jnp.maximum(denom, 1.0), (base, 128))

    pltpu.make_async_copy(recv, recv, data_r).wait()

    early = jnp.concatenate([recv[:, 0].reshape(n * 8, 128), recv[:, 1].reshape(n * 8, 128)], axis=1)
    numer = dot(hot_a[...], early)
    late = dot(hot_b[...], recv[:, 2].reshape(n * 8, 128))
    numer = (numer[:, :128] + late[:base], numer[:, 128:] + late[base:])
    sign = jnp.where(iota((base, 128), 1) < sets, 1.0, -1.0)
    for m in range(mwin):
        stacked = numer[m] / bottom[...]
        swapped = jnp.concatenate([stacked[:, sets:], stacked[:, :sets]], axis=1) * sign
        for r, half in enumerate((stacked, swapped)):
            high = half.astype(BF16)
            right[m, r * base:(r + 1) * base, :128] = high
            right[m, (2 + r) * base:(3 + r) * base, :128] = high
            right[m, r * base:(r + 1) * base, 128:] = (half - high.astype(F32)).astype(BF16)

    step_modes = min(256, modes // 2)
    step_blocks = step_modes // 8

    def project(parity, to):
        for m in range(mwin):
            def step(i, carry, m=m):
                at = pl.ds(pl.multiple_of(i * step_modes, step_modes), step_modes)
                both = dot(beam_t[m, parity, at, :], right[m])
                sums = both[:, :128] + both[:, 128:]
                part[to, pl.ds(i * step_blocks, step_blocks), :, m * 128:(m + 1) * 128] = sums.reshape(step_blocks, 8, 128)
                return carry

            lax.fori_loop(0, modes // 2 // step_modes, step, 0)

    project(1 - core, 0)
    to_core = pltpu.make_async_remote_copy(
        part.at[0], core_recv, core_s, core_r,
        device_id={"chan": chan, "pair": chip * 2 + 1 - core}, device_id_type=MESH)
    to_core.start()
    project(core, 1)
    to_core.wait_recv()

    def merge(i, top):
        at = pl.ds(i * step_chips, step_chips)
        sums = part[1, at] + core_recv[at]
        part[1, at] = sums
        return jnp.maximum(top, jnp.max(jnp.abs(sums), axis=0))

    top = lax.fori_loop(0, chips // step_chips, merge, jnp.zeros((8, columns), F32))
    peak = jnp.max(jnp.max(top, axis=1, keepdims=True), axis=0, keepdims=True)
    peak = jnp.maximum(peak, 1e-30)
    scale_send[...] = jnp.broadcast_to(peak * (1.0 / 32000.0), (1, 128))
    factor = jnp.broadcast_to(32000.0 / peak, (8, columns))

    def code_sums(i, carry):
        at = pl.ds(i * step_chips, step_chips)
        send2[at] = jnp.round(part[1, at] * factor).astype(I32).astype(I16)
        return carry

    lax.fori_loop(0, chips // step_chips, code_sums, 0)

    own_scale = pltpu.make_async_copy(scale_send, scale_recv.at[chip], scale_r)
    own_scale.start()
    own_red = pltpu.make_async_copy(send2.at[chip], recv2.at[chip], red_r)
    own_red.start()

    def send_red(peer):
        target = {"chan": chan, "pair": peer * 2 + core}
        pltpu.make_async_remote_copy(
            send2.at[peer], recv2.at[chip], red_s, red_r, device_id=target, device_id_type=MESH).start()
        pltpu.make_async_remote_copy(
            scale_send, scale_recv.at[chip], scale_s, scale_r, device_id=target, device_id_type=MESH).start()

    each_chip(send_red)
    pltpu.make_async_copy(scale_recv, scale_recv, scale_r).wait()
    pltpu.make_async_copy(recv2, recv2, red_r).wait()

    step_adds = min(8, chips)

    def add_up(i, sums):
        for j in range(step_adds):
            scale = scale_recv[i * step_adds + j]
            sums = sums + recv2[i * step_adds + j].astype(I32).astype(F32) * jnp.concatenate([scale, scale], axis=1)
        return sums

    total = lax.fori_loop(0, chips // step_adds, add_up, jnp.zeros((8, columns), F32))
    modes_ref[...] = total
    square = total * total
    power_0 = jnp.sum(square[:, :128], axis=1, keepdims=True)
    power_1 = jnp.sum(square[:, 128:], axis=1, keepdims=True)
    pow_send[...] = jnp.where(iota((8, 128), 1) == 0, power_0, power_1)
    pow_recv[chan] = pow_send[...]
    sends = []
    for i in range(1, nchan):
        peer = lax.rem(chan + i, nchan)
        copy = pltpu.make_async_remote_copy(
            pow_send, pow_recv.at[chan], pow_s.at[i], pow_r.at[i],
            device_id={"chan": peer, "pair": me}, device_id_type=MESH)
        copy.start()
        sends.append(copy)
    for copy in sends:
        copy.wait()
    power = jnp.sum(pow_recv[...], axis=0) * (1.0 / (nchan * sets))
    power_ref[...] = power[:, :2]

    to_core.wait_send()
    pltpu.make_async_copy(meta_send.at[pl.ds(1, n - 1)], meta_send.at[pl.ds(1, n - 1)], meta_s).wait()
    pltpu.make_async_copy(send.at[pl.ds(1, n - 1)], send.at[pl.ds(1, n - 1)], data_s).wait()
    pltpu.make_async_copy(send2.at[pl.ds(1, chips - 1)], send2.at[pl.ds(1, chips - 1)], red_s).wait()
    pltpu.make_async_copy(scale_recv.at[pl.ds(1, chips - 1)], scale_recv.at[pl.ds(1, chips - 1)], scale_s).wait()


def per_device(visibility, pair_counts, owner_ids, slot_ids, beam):
    n, nchan = lax.axis_size("pair"), lax.axis_size("chan")
    rows, columns = visibility.shape[1:]
    mwin, _, base, modes = beam.shape[1:]
    sets = columns // (2 * mwin)
    chips = n // 2
    vmem, hbm = pl.BlockSpec(memory_space=pltpu.VMEM), pl.BlockSpec(memory_space=pltpu.HBM)
    dma = pltpu.SemaphoreType.DMA
    amplitudes, power = pl.pallas_call(
        functools.partial(body, n, nchan, sets),
        out_shape=(
            jax.ShapeDtypeStruct((8, columns), F32),
            jax.ShapeDtypeStruct((8, mwin), F32),
        ),
        in_specs=[hbm] * 5,
        out_specs=(vmem, vmem),
        scratch_shapes=[
            pltpu.VMEM((1, rows), I32),
            pltpu.VMEM((1, rows), I32),
            pltpu.VMEM((1, rows), I32),
            pltpu.VMEM((rows, columns), BF16),
            pltpu.VMEM((n, 3, 8, 128), BF16),
            pltpu.VMEM((n, 3, 8, 128), BF16),
            pltpu.VMEM((n, 1, 128), F32),
            pltpu.VMEM((n, 1, 128), F32),
            pltpu.VMEM((mwin, 2, base, modes), F32),
            pltpu.VMEM((mwin, 2, modes // 2, 4 * base), BF16),
            pltpu.VMEM((base, n * 8), BF16),
            pltpu.VMEM((2 * base, n * 8), BF16),
            pltpu.VMEM((base, 128), F32),
            pltpu.VMEM((mwin, 4 * base, 256), BF16),
            pltpu.VMEM((2, chips, 8, columns), F32),
            pltpu.VMEM((chips, 8, columns), F32),
            pltpu.VMEM((chips, 8, columns), I16),
            pltpu.VMEM((chips, 8, columns), I16),
            pltpu.VMEM((1, 128), F32),
            pltpu.VMEM((chips, 1, 128), F32),
            pltpu.VMEM((8, 128), F32),
            pltpu.VMEM((nchan, 8, 128), F32),
            dma((4,)), dma, dma, dma, dma, dma, dma, dma, dma, dma, dma, dma,
            dma((nchan,)), dma((nchan,)),
        ],
        compiler_params=pltpu.CompilerParams(
            collective_id=0, has_side_effects=True
        ),
        name="stack_project",
    )(
        owner_ids.reshape(1, rows), slot_ids.reshape(1, rows), pair_counts.reshape(1, rows),
        visibility[0], beam[0],
    )
    return amplitudes.reshape(1, 8, mwin, 2, sets), power


def solution(mesh):
    in_specs = (
        P("chan", "pair", None),
        P("pair"),
        P("pair", None),
        P("pair"),
        P("chan", None, None, "pair", None),
    )
    out_specs = (P("chan", "pair", None, None, None), P("pair", None))
    return jax.shard_map(
        per_device, mesh=mesh, in_specs=in_specs, out_specs=out_specs, check_vma=False
    )
```

```python
import functools

import jax
import jax.numpy as jnp
from jax import lax
from jax.experimental import pallas as pl
from jax.experimental.pallas import tpu as pltpu
from jax.sharding import PartitionSpec as P

MESH = pl.DeviceIdType.MESH
F32, BF16, I32, I16 = jnp.float32, jnp.bfloat16, jnp.int32, jnp.int16


def iota(shape, axis):
    return lax.broadcasted_iota(I32, shape, axis)


def dot(a, b):
    return jnp.dot(a, b, preferred_element_type=F32)


def dot_nt(a, b):
    return lax.dot_general(a, b, (((1,), (1,)), ((), ())), preferred_element_type=F32)


def body(
    n, nchan, sets,
    owner_hbm, slot_hbm, count_hbm, vis_hbm, beam_hbm,
    result_ref,
    owner_ref, slot_ref, count_ref, vis_ref,
    send, recv, meta_send, meta_recv,
    beam_buf, beam_t, hot_a, hot_b, bottom, right,
    part, core_recv, send2, recv2, scale_send, scale_recv, pow_send, pow_recv,
    in_sem, beam_sem, meta_s, meta_r, hand_s, hand_r, data_s, data_r, core_s, core_r, red_s, red_r, scale_s, scale_r, pow_s, pow_r,
):
    chan = lax.axis_index("chan")
    me = lax.axis_index("pair")
    chips = n // 2
    chip, core = me // 2, me % 2
    rows, columns = vis_ref.shape
    step_chips = min(8, chips)

    loads = [
        pltpu.make_async_copy(src, dst, in_sem.at[i])
        for i, (src, dst) in enumerate((
            (owner_hbm, owner_ref), (slot_hbm, slot_ref), (count_hbm, count_ref), (vis_hbm, vis_ref),
        ))
    ]
    for load in loads:
        load.start()
    beam_copy = pltpu.make_async_copy(beam_hbm, beam_buf, beam_sem)
    beam_copy.start()

    barrier = pltpu.get_barrier_semaphore()

    side = 8
    while side * side > chips:
        side //= 2
    depth = chips // side
    chip_row, chip_spot = lax.div(chip, side), lax.rem(chip, side)

    def far(k, size):
        half = lax.div(k, 2) if not isinstance(k, int) else k // 2
        return size // 2 + half - (k - 2 * half) * (2 * half + 1)

    def each_chip(visit):
        along = [lax.rem(chip_spot + far(k, side), side) for k in range(side)]

        def ring(k, carry):
            first = lax.rem(chip_row + far(k, depth), depth) * side
            for step in along:
                visit(first + step)
            return carry

        for step in along[:-1]:
            visit(chip_row * side + step)
        lax.fori_loop(0, depth - 1, ring, 0)

    def greet(pair):
        pl.semaphore_signal(barrier, inc=1, device_id={"chan": chan, "pair": pair}, device_id_type=MESH)

    def greet_chip(peer):
        greet(peer * 2)
        greet(peer * 2 + 1)

    each_chip(greet_chip)
    greet(chip * 2 + 1 - core)
    for i in range(1, nchan):
        peer = lax.rem(chan + i, nchan)
        pl.semaphore_signal(barrier, inc=1, device_id={"chan": peer, "pair": me}, device_id_type=MESH)

    for load in loads:
        load.wait()

    owner = owner_ref[...]
    count = count_ref[...].astype(F32)
    slot = slot_ref[...].astype(F32)
    own_hot = jnp.where(iota((n, rows), 0) == owner, 1.0, 0.0).astype(BF16)
    before = jnp.where(iota((rows, rows), 0) < iota((rows, rows), 1), 1.0, 0.0).astype(BF16)
    rank = jnp.sum(own_hot.astype(F32) * dot(own_hot, before), axis=0, keepdims=True).astype(I32)

    lane_hit = iota((128, rows), 0) == rank
    by_slot = jnp.where(lane_hit, slot, 0.0).astype(BF16)
    by_count = jnp.where(lane_hit, count * 128.0, 0.0).astype(BF16)
    meta = dot_nt(own_hot, by_slot) + dot_nt(own_hot, by_count)
    meta_send[...] = meta.reshape(n, 1, 128)

    target_a = jnp.where(rank < 8, owner * 8 + rank, -1)
    target_b = jnp.where(rank >= 8, owner * 8 + rank - 8, -1)
    step_owners = min(16, n)
    step_rows = step_owners * 8

    def pack(i, carry):
        place = iota((step_rows, rows), 0) + i * step_rows
        pick_a = jnp.where(place == target_a, count, 0.0).astype(BF16)
        pick_b = jnp.where((place & -5) == target_b, count, 0.0).astype(BF16)
        vis = vis_ref[...]
        got_a = dot(pick_a, vis)
        got_b = dot(pick_b, vis)
        low = (iota((step_rows, 128), 0) & 4) == 0
        mixed = jnp.where(low, got_b[:, :128], got_b[:, 128:])
        at = pl.ds(i * step_owners, step_owners)
        send[at, 0] = got_a[:, :128].reshape(step_owners, 8, 128).astype(BF16)
        send[at, 1] = got_a[:, 128:].reshape(step_owners, 8, 128).astype(BF16)
        send[at, 2] = mixed.reshape(step_owners, 8, 128).astype(BF16)
        return carry

    lax.fori_loop(0, n // step_owners, pack, 0)

    pl.semaphore_wait(barrier, n - 1 + nchan - 1)

    def send_meta(pair):
        pltpu.make_async_remote_copy(
            meta_send.at[pair], meta_recv.at[me], meta_s, meta_r,
            device_id={"chan": chan, "pair": pair}, device_id_type=MESH).start()

    groups = chips // nchan
    group = lax.div(chip, nchan)
    keeper = lax.rem(chip, nchan) == chan

    def send_metas(i, carry):
        peer = lax.rem(group + i, groups) * nchan + chan
        send_meta(peer * 2)
        send_meta(peer * 2 + 1)
        return carry

    lax.fori_loop(1, groups, send_metas, 0)

    @pl.when(keeper)
    def _():
        send_meta(chip * 2 + 1 - core)
        pltpu.make_async_copy(meta_send.at[me], meta_recv.at[me], meta_r).start()

    @pl.when(jnp.logical_not(keeper))
    def _():
        send_meta((group * nchan + chan) * 2)
        send_meta((group * nchan + chan) * 2 + 1)

    own_data = pltpu.make_async_copy(send.at[me], recv.at[me], data_r)
    own_data.start()

    def ship(peer):
        pltpu.make_async_remote_copy(
            send.at[peer], recv.at[me], data_s, data_r,
            device_id={"chan": chan, "pair": peer}, device_id_type=MESH).start()

    def ship_chip(peer):
        ship(peer * 2 + core)
        ship(peer * 2 + 1 - core)

    each_chip(ship_chip)
    ship(chip * 2 + 1 - core)

    beam_copy.wait()
    mwin, modes = beam_buf.shape[0], beam_buf.shape[3]
    base = beam_buf.shape[2]
    width = min(128, modes)
    turned = width // 2
    for m in range(mwin):
        for r in range(2):
            def turn(i, carry, m=m, r=r):
                at = pl.ds(pl.multiple_of(i * width, width), width)
                full = jnp.transpose(beam_buf[m, r, :, at])
                high = full.astype(BF16).astype(F32)
                low = full - high
                high, low = high.reshape(width // 16, 2, 8, base), low.reshape(width // 16, 2, 8, base)
                to = pl.ds(pl.multiple_of(i * turned, turned), turned)
                for half in range(2):
                    beam_t[m, half, to, r * base:(r + 1) * base] = high[:, half].reshape(turned, base).astype(BF16)
                    beam_t[m, half, to, (2 + r) * base:(3 + r) * base] = low[:, half].reshape(turned, base).astype(BF16)
                return carry

            lax.fori_loop(0, modes // width, turn, 0)

    right[:, 2 * base:, 128:] = jnp.zeros((mwin, 2 * base, 128), BF16)

    @pl.when(keeper)
    def _():
        pltpu.make_async_copy(meta_recv, meta_recv, meta_r).wait()
        for i in range(1, nchan):
            pltpu.make_async_remote_copy(
                meta_recv, meta_recv, hand_s.at[i], hand_r,
                device_id={"chan": lax.rem(chan + i, nchan), "pair": me}, device_id_type=MESH).start()

    @pl.when(jnp.logical_not(keeper))
    def _():
        pltpu.make_async_copy(meta_recv, meta_recv, hand_r).wait()

    code = jnp.transpose(meta_recv[...].reshape(n, 128))[:16]
    weight = jnp.floor(code * (1.0 / 128.0))
    place = code - weight * 128.0
    both = jnp.concatenate([place, weight], axis=0).astype(BF16)
    spread = dot(both, jnp.where(iota((n, n * 8), 0) == iota((n, n * 8), 1) // 8, 1.0, 0.0).astype(BF16))
    ranks = iota((16, n * 8), 0)
    in_message = iota((16, n * 8), 1) & 7
    at_a = ranks == in_message
    at_b = ranks == 8 + (in_message & 3)

    def flat(values, mask):
        return jnp.sum(jnp.where(mask, values, 0.0), axis=0, keepdims=True)

    slot_a, slot_b = flat(spread[:16], at_a), flat(spread[:16], at_b)
    weight_a, weight_b = flat(spread[16:], at_a), flat(spread[16:], at_b)
    bases = iota((base, n * 8), 0).astype(F32)
    first = (iota((base, n * 8), 1) & 4) == 0
    hit_a = jnp.where(bases == slot_a, 1.0, 0.0)
    hit_b = jnp.where(bases == slot_b, 1.0, 0.0)
    hot_a[...] = hit_a.astype(BF16)
    hot_b[:base] = jnp.where(first, hit_b, 0.0).astype(BF16)
    hot_b[base:] = jnp.where(first, 0.0, hit_b).astype(BF16)
    denom = jnp.sum(hit_a * weight_a + jnp.where(first, hit_b, 0.0) * weight_b, axis=1, keepdims=True)
    bottom[...] = jnp.broadcast_to(jnp.maximum(denom, 1.0), (base, 128))

    pltpu.make_async_copy(recv, recv, data_r).wait()

    early = jnp.concatenate([recv[:, 0].reshape(n * 8, 128), recv[:, 1].reshape(n * 8, 128)], axis=1)
    numer = dot(hot_a[...], early)
    late = dot(hot_b[...], recv[:, 2].reshape(n * 8, 128))
    numer = (numer[:, :128] + late[:base], numer[:, 128:] + late[base:])
    sign = jnp.where(iota((base, 128), 1) < sets, 1.0, -1.0)
    for m in range(mwin):
        stacked = numer[m] / bottom[...]
        swapped = jnp.concatenate([stacked[:, sets:], stacked[:, :sets]], axis=1) * sign
        for r, half in enumerate((stacked, swapped)):
            high = half.astype(BF16)
            right[m, r * base:(r + 1) * base, :128] = high
            right[m, (2 + r) * base:(3 + r) * base, :128] = high
            right[m, r * base:(r + 1) * base, 128:] = (half - high.astype(F32)).astype(BF16)

    step_modes = min(256, modes // 2)
    step_blocks = step_modes // 8

    def project(parity, to, m):
        def step(i, carry):
            at = pl.ds(pl.multiple_of(i * step_modes, step_modes), step_modes)
            both = dot(beam_t[m, parity, at, :], right[m])
            sums = both[:, :128] + both[:, 128:]
            part[to, m, pl.ds(i * step_blocks, step_blocks)] = sums.reshape(step_blocks, 8, 128)
            return carry

        lax.fori_loop(0, modes // 2 // step_modes, step, 0)

    to_core = []
    for m in range(mwin):
        project(1 - core, 0, m)
        to_core.append(pltpu.make_async_remote_copy(
            part.at[0, m], core_recv.at[m], core_s.at[m], core_r.at[m],
            device_id={"chan": chan, "pair": chip * 2 + 1 - core}, device_id_type=MESH))
        to_core[m].start()
    for m in range(mwin):
        project(core, 1, m)
    for m in range(mwin):
        to_core[m].wait_recv()

    def merge(i, top):
        at = pl.ds(i * step_chips, step_chips)
        for m in range(mwin):
            sums = part[1, m, at] + core_recv[m, at]
            part[1, m, at] = sums
            top = jnp.maximum(top, jnp.max(jnp.abs(sums), axis=0))
        return top

    top = lax.fori_loop(0, chips // step_chips, merge, jnp.zeros((8, 128), F32))
    peak = jnp.max(jnp.max(top, axis=1, keepdims=True), axis=0, keepdims=True)
    peak = jnp.maximum(peak, 1e-30)
    scale_send[...] = jnp.broadcast_to(peak * (1.0 / 32000.0), (1, 128))
    factor = jnp.broadcast_to(32000.0 / peak, (8, 128))

    def code_sums(i, carry):
        at = pl.ds(i * step_chips, step_chips)
        scaled = jnp.concatenate([part[1, 0, at] * factor, part[1, 1, at] * factor], axis=2)
        send2[at] = jnp.round(scaled).astype(I32).astype(I16)
        return carry

    lax.fori_loop(0, chips // step_chips, code_sums, 0)

    own_scale = pltpu.make_async_copy(scale_send, scale_recv.at[chip], scale_r)
    own_scale.start()
    own_red = pltpu.make_async_copy(send2.at[chip], recv2.at[chip], red_r)
    own_red.start()

    def send_red(peer):
        target = {"chan": chan, "pair": peer * 2 + core}
        pltpu.make_async_remote_copy(
            send2.at[peer], recv2.at[chip], red_s, red_r, device_id=target, device_id_type=MESH).start()
        pltpu.make_async_remote_copy(
            scale_send, scale_recv.at[chip], scale_s, scale_r, device_id=target, device_id_type=MESH).start()

    each_chip(send_red)
    pltpu.make_async_copy(scale_recv, scale_recv, scale_r).wait()
    pltpu.make_async_copy(recv2, recv2, red_r).wait()

    step_adds = min(8, chips)

    def add_up(i, sums):
        for j in range(step_adds):
            scale = scale_recv[i * step_adds + j]
            sums = sums + recv2[i * step_adds + j].astype(I32).astype(F32) * jnp.concatenate([scale, scale], axis=1)
        return sums

    total = lax.fori_loop(0, chips // step_adds, add_up, jnp.zeros((8, columns), F32))
    result_ref[:, :columns] = total
    square = total * total
    power_0 = jnp.sum(square[:, :128], axis=1, keepdims=True)
    power_1 = jnp.sum(square[:, 128:], axis=1, keepdims=True)
    pow_send[...] = jnp.where(iota((8, 128), 1) == 0, power_0, power_1)
    pow_recv[chan] = pow_send[...]
    sends = []
    for i in range(1, nchan):
        peer = lax.rem(chan + i, nchan)
        copy = pltpu.make_async_remote_copy(
            pow_send, pow_recv.at[chan], pow_s.at[i], pow_r.at[i],
            device_id={"chan": peer, "pair": me}, device_id_type=MESH)
        copy.start()
        sends.append(copy)
    for copy in sends:
        copy.wait()
    power = jnp.sum(pow_recv[...], axis=0) * (1.0 / (nchan * sets))
    result_ref[:, columns:] = power

    for copy in to_core:
        copy.wait_send()
    sent = 2 * groups

    @pl.when(keeper)
    def _():
        pltpu.make_async_copy(meta_send.at[pl.ds(0, sent - 1)], meta_send.at[pl.ds(0, sent - 1)], meta_s).wait()
        for i in range(1, nchan):
            pltpu.make_async_copy(meta_recv, meta_recv, hand_s.at[i]).wait()

    @pl.when(jnp.logical_not(keeper))
    def _():
        pltpu.make_async_copy(meta_send.at[pl.ds(0, sent)], meta_send.at[pl.ds(0, sent)], meta_s).wait()

    pltpu.make_async_copy(send.at[pl.ds(1, n - 1)], send.at[pl.ds(1, n - 1)], data_s).wait()
    pltpu.make_async_copy(send2.at[pl.ds(1, chips - 1)], send2.at[pl.ds(1, chips - 1)], red_s).wait()
    pltpu.make_async_copy(scale_recv.at[pl.ds(1, chips - 1)], scale_recv.at[pl.ds(1, chips - 1)], scale_s).wait()


def shape_results(mwin, sets, result_ref, modes_ref, power_ref):
    for m in range(mwin):
        for part in range(2):
            at = (2 * m + part) * sets
            modes_ref[:, m, part, :] = result_ref[:, at:at + sets]
    power_ref[...] = jnp.transpose(result_ref[:, 2 * mwin * sets:])[:mwin]


def per_device(visibility, pair_counts, owner_ids, slot_ids, beam):
    n, nchan = lax.axis_size("pair"), lax.axis_size("chan")
    rows, columns = visibility.shape[1:]
    mwin, _, base, modes = beam.shape[1:]
    sets = columns // (2 * mwin)
    chips = n // 2
    vmem, hbm = pl.BlockSpec(memory_space=pltpu.VMEM), pl.BlockSpec(memory_space=pltpu.HBM)
    dma = pltpu.SemaphoreType.DMA
    result = pl.pallas_call(
        functools.partial(body, n, nchan, sets),
        out_shape=jax.ShapeDtypeStruct((8, columns + 128), F32),
        in_specs=[hbm] * 5,
        out_specs=vmem,
        scratch_shapes=[
            pltpu.VMEM((1, rows), I32),
            pltpu.VMEM((1, rows), I32),
            pltpu.VMEM((1, rows), I32),
            pltpu.VMEM((rows, columns), BF16),
            pltpu.VMEM((n, 3, 8, 128), BF16),
            pltpu.VMEM((n, 3, 8, 128), BF16),
            pltpu.VMEM((n, 1, 128), F32),
            pltpu.VMEM((n, 1, 128), F32),
            pltpu.VMEM((mwin, 2, base, modes), F32),
            pltpu.VMEM((mwin, 2, modes // 2, 4 * base), BF16),
            pltpu.VMEM((base, n * 8), BF16),
            pltpu.VMEM((2 * base, n * 8), BF16),
            pltpu.VMEM((base, 128), F32),
            pltpu.VMEM((mwin, 4 * base, 256), BF16),
            pltpu.VMEM((2, mwin, chips, 8, 128), F32),
            pltpu.VMEM((mwin, chips, 8, 128), F32),
            pltpu.VMEM((chips, 8, columns), I16),
            pltpu.VMEM((chips, 8, columns), I16),
            pltpu.VMEM((1, 128), F32),
            pltpu.VMEM((chips, 1, 128), F32),
            pltpu.VMEM((8, 128), F32),
            pltpu.VMEM((nchan, 8, 128), F32),
            dma((4,)), dma, dma, dma, dma((nchan,)), dma, dma, dma, dma((mwin,)), dma((mwin,)), dma, dma, dma, dma,
            dma((nchan,)), dma((nchan,)),
        ],
        compiler_params=pltpu.CompilerParams(
            collective_id=0, has_side_effects=True
        ),
        name="stack_project",
    )(
        owner_ids.reshape(1, rows), slot_ids.reshape(1, rows), pair_counts.reshape(1, rows),
        visibility[0], beam[0],
    )
    shaped, power = pl.pallas_call(
        functools.partial(shape_results, mwin, sets),
        out_shape=(jax.ShapeDtypeStruct((8, mwin, 2, sets), F32), jax.ShapeDtypeStruct((mwin, 8), F32)),
        in_specs=[vmem],
        out_specs=(vmem, vmem),
        name="shape_results",
    )(result)
    return shaped[None], power.T


def solution(mesh):
    in_specs = (
        P("chan", "pair", None),
        P("pair"),
        P("pair", None),
        P("pair"),
        P("chan", None, None, "pair", None),
    )
    out_specs = (P("chan", "pair", None, None, None), P("pair", None))
    return jax.shard_map(
        per_device, mesh=mesh, in_specs=in_specs, out_specs=out_specs, check_vma=False
    )
```

```python
import functools

import jax
import jax.numpy as jnp
from jax import lax
from jax.experimental import pallas as pl
from jax.experimental.pallas import tpu as pltpu
from jax.sharding import PartitionSpec as P

MESH = pl.DeviceIdType.MESH
F32, BF16, I32, I16 = jnp.float32, jnp.bfloat16, jnp.int32, jnp.int16


def iota(shape, axis):
    return lax.broadcasted_iota(I32, shape, axis)


def dot(a, b):
    return jnp.dot(a, b, preferred_element_type=F32)


def dot_nt(a, b):
    return lax.dot_general(a, b, (((1,), (1,)), ((), ())), preferred_element_type=F32)


def ring_size(chips):
    side = 8
    while side * side > chips:
        side //= 2
    return side


def body(
    n, nchan, sets,
    owner_hbm, slot_hbm, count_hbm, vis_hbm, beam_hbm,
    result_ref,
    owner_ref, slot_ref, count_ref, vis_ref,
    send, recv, meta_send, meta_recv,
    beam_buf, beam_t, hot_a, hot_b, bottom, right,
    part, core_recv, send2, recv2, scale_send, scale_recv, pow_send, pow_recv,
    hellos, in_sem, beam_sem, meta_s, meta_r, hand_s, hand_r, data_s, data_r, core_s, core_r, red_s, red_r, scale_s, scale_r, pow_s, pow_r,
):
    chan = lax.axis_index("chan")
    me = lax.axis_index("pair")
    chips = n // 2
    chip, core = me // 2, me % 2
    rows, columns = vis_ref.shape
    step_chips = min(8, chips)

    loads = [
        pltpu.make_async_copy(src, dst, in_sem.at[i])
        for i, (src, dst) in enumerate((
            (owner_hbm, owner_ref), (slot_hbm, slot_ref), (count_hbm, count_ref), (vis_hbm, vis_ref),
        ))
    ]
    for load in loads:
        load.start()
    beam_copy = pltpu.make_async_copy(beam_hbm, beam_buf, beam_sem)
    beam_copy.start()

    barrier = pltpu.get_barrier_semaphore()

    side = ring_size(chips)
    depth = chips // side
    chip_row, chip_spot = lax.div(chip, side), lax.rem(chip, side)

    def far(k, size):
        half = lax.div(k, 2) if not isinstance(k, int) else k // 2
        return size // 2 + half - (k - 2 * half) * (2 * half + 1)

    def each_chip(visit):
        along = [lax.rem(chip_spot + far(k, side), side) for k in range(side)]

        def ring(k, carry):
            first = lax.rem(chip_row + far(k, depth), depth) * side
            for step in along:
                visit(first + step)
            return carry

        for step in along[:-1]:
            visit(chip_row * side + step)
        lax.fori_loop(0, depth - 1, ring, 0)

    group_size = depth * 2
    my_place = chip_row * 2 + core

    def pair_at(spot, line, which):
        return (line * side + spot) * 2 + which

    def greet(sem, pair):
        pl.semaphore_signal(sem, inc=1, device_id={"chan": chan, "pair": pair}, device_id_type=MESH)

    def greet_group(sem, spot):
        for line in range(depth):
            for which in range(2):
                greet(sem, pair_at(spot, line, which))

    def greet_later(spot, carry):
        greet_group(barrier, spot)
        return carry

    def greet_own(sem):
        def line_of(line, carry):
            greet(sem, pair_at(chip_spot, line, 0))
            greet(sem, pair_at(chip_spot, line, 1))
            return carry
        return line_of

    @pl.when(core == 0)
    def _():
        greet(barrier, me + 1)

    lax.fori_loop(chip_row + 1, depth, greet_own(barrier), 0)
    for i in range(1, nchan):
        peer = lax.rem(chan + i, nchan)
        pl.semaphore_signal(barrier, inc=1, device_id={"chan": peer, "pair": me}, device_id_type=MESH)
    lax.fori_loop(chip_spot + 1, side, greet_later, 0)

    pl.semaphore_wait(barrier, chip_spot * group_size + my_place + nchan - 1)

    hello = hellos.at[chip_spot]

    @pl.when(core == 1)
    def _():
        greet(hello, me - 1)

    lax.fori_loop(0, chip_row, greet_own(hello), 0)

    def greet_earlier(i, carry):
        greet_group(hello, chip_spot - i)
        return carry

    lax.fori_loop(1, chip_spot + 1, greet_earlier, 0)

    for load in loads:
        load.wait()

    owner = owner_ref[...]
    count = count_ref[...].astype(F32)
    slot = slot_ref[...].astype(F32)
    own_hot = jnp.where(iota((n, rows), 0) == owner, 1.0, 0.0).astype(BF16)
    before = jnp.where(iota((rows, rows), 0) < iota((rows, rows), 1), 1.0, 0.0).astype(BF16)
    rank = jnp.sum(own_hot.astype(F32) * dot(own_hot, before), axis=0, keepdims=True).astype(I32)

    lane_hit = iota((128, rows), 0) == rank
    by_slot = jnp.where(lane_hit, slot, 0.0).astype(BF16)
    by_count = jnp.where(lane_hit, count * 128.0, 0.0).astype(BF16)
    meta = dot_nt(own_hot, by_slot) + dot_nt(own_hot, by_count)
    meta_send[...] = meta.reshape(n, 1, 128)

    target_a = jnp.where(rank < 8, owner * 8 + rank, -1)
    target_b = jnp.where(rank >= 8, owner * 8 + rank - 8, -1)
    step_owners = min(16, n)
    step_rows = step_owners * 8

    def pack(i, carry):
        place = iota((step_rows, rows), 0) + i * step_rows
        pick_a = jnp.where(place == target_a, count, 0.0).astype(BF16)
        pick_b = jnp.where((place & -5) == target_b, count, 0.0).astype(BF16)
        vis = vis_ref[...]
        got_a = dot(pick_a, vis)
        got_b = dot(pick_b, vis)
        low = (iota((step_rows, 128), 0) & 4) == 0
        mixed = jnp.where(low, got_b[:, :128], got_b[:, 128:])
        at = pl.ds(i * step_owners, step_owners)
        send[at, 0] = got_a[:, :128].reshape(step_owners, 8, 128).astype(BF16)
        send[at, 1] = got_a[:, 128:].reshape(step_owners, 8, 128).astype(BF16)
        send[at, 2] = mixed.reshape(step_owners, 8, 128).astype(BF16)
        return carry

    lax.fori_loop(0, n // step_owners, pack, 0)

    keeper = lax.rem(chip_spot, nchan) == chan

    def ship(pair):
        pltpu.make_async_remote_copy(
            send.at[pair], recv.at[me], data_s, data_r,
            device_id={"chan": chan, "pair": pair}, device_id_type=MESH).start()

    def ship_meta(pair):
        pltpu.make_async_remote_copy(
            meta_send.at[pair], meta_recv.at[me], meta_s, meta_r,
            device_id={"chan": chan, "pair": pair}, device_id_type=MESH).start()

    lines = [lax.rem(chip_row + far(k, depth), depth) for k in range(depth)]

    def ship_group(spot, own):
        def every(visit):
            for line in lines[:depth - 1 if own else depth]:
                visit(pair_at(spot, line, core))
                visit(pair_at(spot, line, 1 - core))
            if own:
                visit(chip * 2 + 1 - core)

        @pl.when(lax.rem(spot, nchan) == chan)
        def _():
            every(ship_meta)

        every(ship)

    def ship_earlier(i, carry):
        ship_group(chip_spot - i, False)
        return carry

    def ship_later(spot, carry):
        pl.semaphore_wait(hellos.at[spot], group_size)
        ship_group(spot, False)
        return carry

    @pl.when(keeper)
    def _():
        pltpu.make_async_copy(meta_send.at[me], meta_recv.at[me], meta_r).start()

    own_data = pltpu.make_async_copy(send.at[me], recv.at[me], data_r)
    own_data.start()
    lax.fori_loop(1, chip_spot + 1, ship_earlier, 0)

    @pl.when(my_place < group_size - 1)
    def _():
        pl.semaphore_wait(hello, group_size - 1 - my_place)

    ship_group(chip_spot, True)
    lax.fori_loop(chip_spot + 1, side, ship_later, 0)

    beam_copy.wait()
    mwin, modes = beam_buf.shape[0], beam_buf.shape[3]
    base = beam_buf.shape[2]
    width = min(128, modes)
    turned = width // 2
    for m in range(mwin):
        for r in range(2):
            def turn(i, carry, m=m, r=r):
                at = pl.ds(pl.multiple_of(i * width, width), width)
                full = jnp.transpose(beam_buf[m, r, :, at])
                high = full.astype(BF16).astype(F32)
                low = full - high
                high, low = high.reshape(width // 16, 2, 8, base), low.reshape(width // 16, 2, 8, base)
                to = pl.ds(pl.multiple_of(i * turned, turned), turned)
                for half in range(2):
                    beam_t[m, half, to, r * base:(r + 1) * base] = high[:, half].reshape(turned, base).astype(BF16)
                    beam_t[m, half, to, (2 + r) * base:(3 + r) * base] = low[:, half].reshape(turned, base).astype(BF16)
                return carry

            lax.fori_loop(0, modes // width, turn, 0)

    right[:, 2 * base:, 128:] = jnp.zeros((mwin, 2 * base, 128), BF16)

    @pl.when(keeper)
    def _():
        pltpu.make_async_copy(meta_recv, meta_recv, meta_r).wait()
        for i in range(1, nchan):
            pltpu.make_async_remote_copy(
                meta_recv, meta_recv, hand_s.at[i], hand_r,
                device_id={"chan": lax.rem(chan + i, nchan), "pair": me}, device_id_type=MESH).start()

    @pl.when(jnp.logical_not(keeper))
    def _():
        pltpu.make_async_copy(meta_recv, meta_recv, hand_r).wait()

    code = jnp.transpose(meta_recv[...].reshape(n, 128))[:16]
    weight = jnp.floor(code * (1.0 / 128.0))
    place = code - weight * 128.0
    both = jnp.concatenate([place, weight], axis=0).astype(BF16)
    spread = dot(both, jnp.where(iota((n, n * 8), 0) == iota((n, n * 8), 1) // 8, 1.0, 0.0).astype(BF16))
    ranks = iota((16, n * 8), 0)
    in_message = iota((16, n * 8), 1) & 7
    at_a = ranks == in_message
    at_b = ranks == 8 + (in_message & 3)

    def flat(values, mask):
        return jnp.sum(jnp.where(mask, values, 0.0), axis=0, keepdims=True)

    slot_a, slot_b = flat(spread[:16], at_a), flat(spread[:16], at_b)
    weight_a, weight_b = flat(spread[16:], at_a), flat(spread[16:], at_b)
    bases = iota((base, n * 8), 0).astype(F32)
    first = (iota((base, n * 8), 1) & 4) == 0
    hit_a = jnp.where(bases == slot_a, 1.0, 0.0)
    hit_b = jnp.where(bases == slot_b, 1.0, 0.0)
    hot_a[...] = hit_a.astype(BF16)
    hot_b[:base] = jnp.where(first, hit_b, 0.0).astype(BF16)
    hot_b[base:] = jnp.where(first, 0.0, hit_b).astype(BF16)
    denom = jnp.sum(hit_a * weight_a + jnp.where(first, hit_b, 0.0) * weight_b, axis=1, keepdims=True)
    bottom[...] = jnp.broadcast_to(jnp.maximum(denom, 1.0), (base, 128))

    pltpu.make_async_copy(recv, recv, data_r).wait()

    early = jnp.concatenate([recv[:, 0].reshape(n * 8, 128), recv[:, 1].reshape(n * 8, 128)], axis=1)
    numer = dot(hot_a[...], early)
    late = dot(hot_b[...], recv[:, 2].reshape(n * 8, 128))
    numer = (numer[:, :128] + late[:base], numer[:, 128:] + late[base:])
    sign = jnp.where(iota((base, 128), 1) < sets, 1.0, -1.0)
    for m in range(mwin):
        stacked = numer[m] / bottom[...]
        swapped = jnp.concatenate([stacked[:, sets:], stacked[:, :sets]], axis=1) * sign
        for r, half in enumerate((stacked, swapped)):
            high = half.astype(BF16)
            right[m, r * base:(r + 1) * base, :128] = high
            right[m, (2 + r) * base:(3 + r) * base, :128] = high
            right[m, r * base:(r + 1) * base, 128:] = (half - high.astype(F32)).astype(BF16)

    step_modes = min(256, modes // 2)
    step_blocks = step_modes // 8

    def project(parity, to, m):
        def step(i, carry):
            at = pl.ds(pl.multiple_of(i * step_modes, step_modes), step_modes)
            both = dot(beam_t[m, parity, at, :], right[m])
            sums = both[:, :128] + both[:, 128:]
            part[to, m, pl.ds(i * step_blocks, step_blocks)] = sums.reshape(step_blocks, 8, 128)
            return carry

        lax.fori_loop(0, modes // 2 // step_modes, step, 0)

    to_core = []
    for m in range(mwin):
        project(1 - core, 0, m)
        to_core.append(pltpu.make_async_remote_copy(
            part.at[0, m], core_recv.at[m], core_s.at[m], core_r.at[m],
            device_id={"chan": chan, "pair": chip * 2 + 1 - core}, device_id_type=MESH))
        to_core[m].start()
    for m in range(mwin):
        project(core, 1, m)
    for m in range(mwin):
        to_core[m].wait_recv()

    def merge(i, top):
        at = pl.ds(i * step_chips, step_chips)
        for m in range(mwin):
            sums = part[1, m, at] + core_recv[m, at]
            part[1, m, at] = sums
            top = jnp.maximum(top, jnp.max(jnp.abs(sums), axis=0))
        return top

    top = lax.fori_loop(0, chips // step_chips, merge, jnp.zeros((8, 128), F32))
    peak = jnp.max(jnp.max(top, axis=1, keepdims=True), axis=0, keepdims=True)
    peak = jnp.maximum(peak, 1e-30)
    scale_send[...] = jnp.broadcast_to(peak * (1.0 / 32000.0), (1, 128))
    factor = jnp.broadcast_to(32000.0 / peak, (8, 128))

    def code_sums(i, carry):
        at = pl.ds(i * step_chips, step_chips)
        scaled = jnp.concatenate([part[1, 0, at] * factor, part[1, 1, at] * factor], axis=2)
        send2[at] = jnp.round(scaled).astype(I32).astype(I16)
        return carry

    lax.fori_loop(0, chips // step_chips, code_sums, 0)

    own_scale = pltpu.make_async_copy(scale_send, scale_recv.at[chip], scale_r)
    own_scale.start()
    own_red = pltpu.make_async_copy(send2.at[chip], recv2.at[chip], red_r)
    own_red.start()

    def send_red(peer):
        target = {"chan": chan, "pair": peer * 2 + core}
        pltpu.make_async_remote_copy(
            send2.at[peer], recv2.at[chip], red_s, red_r, device_id=target, device_id_type=MESH).start()
        pltpu.make_async_remote_copy(
            scale_send, scale_recv.at[chip], scale_s, scale_r, device_id=target, device_id_type=MESH).start()

    each_chip(send_red)
    pltpu.make_async_copy(scale_recv, scale_recv, scale_r).wait()
    pltpu.make_async_copy(recv2, recv2, red_r).wait()

    step_adds = min(8, chips)

    def add_up(i, sums):
        for j in range(step_adds):
            scale = scale_recv[i * step_adds + j]
            sums = sums + recv2[i * step_adds + j].astype(I32).astype(F32) * jnp.concatenate([scale, scale], axis=1)
        return sums

    total = lax.fori_loop(0, chips // step_adds, add_up, jnp.zeros((8, columns), F32))
    result_ref[:, :columns] = total
    square = total * total
    power_0 = jnp.sum(square[:, :128], axis=1, keepdims=True)
    power_1 = jnp.sum(square[:, 128:], axis=1, keepdims=True)
    pow_send[...] = jnp.where(iota((8, 128), 1) == 0, power_0, power_1)
    pow_recv[chan] = pow_send[...]
    sends = []
    for i in range(1, nchan):
        peer = lax.rem(chan + i, nchan)
        copy = pltpu.make_async_remote_copy(
            pow_send, pow_recv.at[chan], pow_s.at[i], pow_r.at[i],
            device_id={"chan": peer, "pair": me}, device_id_type=MESH)
        copy.start()
        sends.append(copy)
    for copy in sends:
        copy.wait()
    power = jnp.sum(pow_recv[...], axis=0) * (1.0 / (nchan * sets))
    result_ref[:, columns:] = power

    for copy in to_core:
        copy.wait_send()
    sent = group_size * (side // nchan)

    @pl.when(keeper)
    def _():
        pltpu.make_async_copy(meta_send.at[pl.ds(0, sent - 1)], meta_send.at[pl.ds(0, sent - 1)], meta_s).wait()
        for i in range(1, nchan):
            pltpu.make_async_copy(meta_recv, meta_recv, hand_s.at[i]).wait()

    @pl.when(jnp.logical_not(keeper))
    def _():
        pltpu.make_async_copy(meta_send.at[pl.ds(0, sent)], meta_send.at[pl.ds(0, sent)], meta_s).wait()

    pltpu.make_async_copy(send.at[pl.ds(1, n - 1)], send.at[pl.ds(1, n - 1)], data_s).wait()
    pltpu.make_async_copy(send2.at[pl.ds(1, chips - 1)], send2.at[pl.ds(1, chips - 1)], red_s).wait()
    pltpu.make_async_copy(scale_recv.at[pl.ds(1, chips - 1)], scale_recv.at[pl.ds(1, chips - 1)], scale_s).wait()


def shape_results(mwin, sets, result_ref, modes_ref, power_ref):
    for m in range(mwin):
        for part in range(2):
            at = (2 * m + part) * sets
            modes_ref[:, m, part, :] = result_ref[:, at:at + sets]
    power_ref[...] = jnp.transpose(result_ref[:, 2 * mwin * sets:])[:mwin]


def per_device(visibility, pair_counts, owner_ids, slot_ids, beam):
    n, nchan = lax.axis_size("pair"), lax.axis_size("chan")
    rows, columns = visibility.shape[1:]
    mwin, _, base, modes = beam.shape[1:]
    sets = columns // (2 * mwin)
    chips = n // 2
    vmem, hbm = pl.BlockSpec(memory_space=pltpu.VMEM), pl.BlockSpec(memory_space=pltpu.HBM)
    dma = pltpu.SemaphoreType.DMA
    result = pl.pallas_call(
        functools.partial(body, n, nchan, sets),
        out_shape=jax.ShapeDtypeStruct((8, columns + 128), F32),
        in_specs=[hbm] * 5,
        out_specs=vmem,
        scratch_shapes=[
            pltpu.VMEM((1, rows), I32),
            pltpu.VMEM((1, rows), I32),
            pltpu.VMEM((1, rows), I32),
            pltpu.VMEM((rows, columns), BF16),
            pltpu.VMEM((n, 3, 8, 128), BF16),
            pltpu.VMEM((n, 3, 8, 128), BF16),
            pltpu.VMEM((n, 1, 128), F32),
            pltpu.VMEM((n, 1, 128), F32),
            pltpu.VMEM((mwin, 2, base, modes), F32),
            pltpu.VMEM((mwin, 2, modes // 2, 4 * base), BF16),
            pltpu.VMEM((base, n * 8), BF16),
            pltpu.VMEM((2 * base, n * 8), BF16),
            pltpu.VMEM((base, 128), F32),
            pltpu.VMEM((mwin, 4 * base, 256), BF16),
            pltpu.VMEM((2, mwin, chips, 8, 128), F32),
            pltpu.VMEM((mwin, chips, 8, 128), F32),
            pltpu.VMEM((chips, 8, columns), I16),
            pltpu.VMEM((chips, 8, columns), I16),
            pltpu.VMEM((1, 128), F32),
            pltpu.VMEM((chips, 1, 128), F32),
            pltpu.VMEM((8, 128), F32),
            pltpu.VMEM((nchan, 8, 128), F32),
            pltpu.SemaphoreType.REGULAR((ring_size(n // 2),)), dma((4,)), dma, dma, dma, dma((nchan,)), dma, dma, dma, dma((mwin,)), dma((mwin,)), dma, dma, dma, dma,
            dma((nchan,)), dma((nchan,)),
        ],
        compiler_params=pltpu.CompilerParams(
            collective_id=0, has_side_effects=True
        ),
        name="stack_project",
    )(
        owner_ids.reshape(1, rows), slot_ids.reshape(1, rows), pair_counts.reshape(1, rows),
        visibility[0], beam[0],
    )
    shaped, power = pl.pallas_call(
        functools.partial(shape_results, mwin, sets),
        out_shape=(jax.ShapeDtypeStruct((8, mwin, 2, sets), F32), jax.ShapeDtypeStruct((mwin, 8), F32)),
        in_specs=[vmem],
        out_specs=(vmem, vmem),
        name="shape_results",
    )(result)
    return shaped[None], power.T


def solution(mesh):
    in_specs = (
        P("chan", "pair", None),
        P("pair"),
        P("pair", None),
        P("pair"),
        P("chan", None, None, "pair", None),
    )
    out_specs = (P("chan", "pair", None, None, None), P("pair", None))
    return jax.shard_map(
        per_device, mesh=mesh, in_specs=in_specs, out_specs=out_specs, check_vma=False
    )
```

```python
import functools

import jax
import jax.numpy as jnp
from jax import lax
from jax.experimental import pallas as pl
from jax.experimental.pallas import tpu as pltpu
from jax.sharding import PartitionSpec as P

MESH = pl.DeviceIdType.MESH
F32, BF16, I32, I16 = jnp.float32, jnp.bfloat16, jnp.int32, jnp.int16


def iota(shape, axis):
    return lax.broadcasted_iota(I32, shape, axis)


def dot(a, b):
    return jnp.dot(a, b, preferred_element_type=F32)


def dot_nt(a, b):
    return lax.dot_general(a, b, (((1,), (1,)), ((), ())), preferred_element_type=F32)


def body(
    n, nchan, sets,
    owner_hbm, slot_hbm, count_hbm, vis_hbm, beam_hbm,
    result_hbm, power_hbm,
    owner_ref, slot_ref, count_ref, vis_ref,
    send, recv, meta_send, meta_recv,
    beam_buf, beam_t, hot_a, hot_b, bottom, right,
    part, core_recv, send2, recv2, scale_send, scale_recv, total_buf, pow_send,
    in_sem, beam_sem, meta_s, meta_r, hand_s, hand_r, data_s, data_r, core_s, core_r, red_s, red_r, scale_s, scale_r, pow_s, pow_r, out_sem, own_sem,
):
    chan = lax.axis_index("chan")
    me = lax.axis_index("pair")
    chips = n // 2
    chip, core = me // 2, me % 2
    rows, columns = vis_ref.shape
    step_chips = min(8, chips)

    loads = [
        pltpu.make_async_copy(src, dst, in_sem.at[i])
        for i, (src, dst) in enumerate((
            (owner_hbm, owner_ref), (slot_hbm, slot_ref), (count_hbm, count_ref), (vis_hbm, vis_ref),
        ))
    ]
    for load in loads:
        load.start()
    beam_copy = pltpu.make_async_copy(beam_hbm, beam_buf, beam_sem)
    beam_copy.start()

    barrier = pltpu.get_barrier_semaphore()

    side = 8
    while side * side > chips:
        side //= 2
    depth = chips // side
    chip_row, chip_spot = lax.div(chip, side), lax.rem(chip, side)

    def far(k, size):
        half = lax.div(k, 2) if not isinstance(k, int) else k // 2
        return size // 2 + half - (k - 2 * half) * (2 * half + 1)

    def each_chip(visit):
        for k in range(side - 1):
            visit(chip_row * side + lax.rem(chip_spot + far(k, side), side))

        def diagonal(total, carry):
            def step(k, carry):
                line = lax.rem(chip_row + far(k, depth), depth)
                visit(line * side + lax.rem(chip_spot + far(total - k, side), side))
                return carry

            return lax.fori_loop(lax.max(0, total - side + 1), lax.min(depth - 1, total + 1), step, carry)

        lax.fori_loop(0, depth + side - 2, diagonal, 0)

    def greet(pair):
        pl.semaphore_signal(barrier, inc=1, device_id={"chan": chan, "pair": pair}, device_id_type=MESH)

    def greet_chip(peer):
        greet(peer * 2)
        greet(peer * 2 + 1)

    each_chip(greet_chip)
    greet(chip * 2 + 1 - core)
    for i in range(1, nchan):
        peer = lax.rem(chan + i, nchan)
        pl.semaphore_signal(barrier, inc=1, device_id={"chan": peer, "pair": me}, device_id_type=MESH)

    for load in loads:
        load.wait()

    owner = owner_ref[...]
    count = count_ref[...].astype(F32)
    slot = slot_ref[...].astype(F32)
    own_hot = jnp.where(iota((n, rows), 0) == owner, 1.0, 0.0).astype(BF16)
    before = jnp.where(iota((rows, rows), 0) < iota((rows, rows), 1), 1.0, 0.0).astype(BF16)
    rank = jnp.sum(own_hot.astype(F32) * dot(own_hot, before), axis=0, keepdims=True).astype(I32)

    lane_hit = iota((128, rows), 0) == rank
    by_slot = jnp.where(lane_hit, slot, 0.0).astype(BF16)
    by_count = jnp.where(lane_hit, count * 128.0, 0.0).astype(BF16)
    meta = dot_nt(own_hot, by_slot) + dot_nt(own_hot, by_count)
    meta_send[...] = meta.reshape(n, 1, 128)

    target_a = jnp.where(rank < 8, owner * 8 + rank, -1)
    target_b = jnp.where(rank >= 8, owner * 8 + rank - 8, -1)
    step_owners = min(16, n)
    step_rows = step_owners * 8

    def pack(i, carry):
        place = iota((step_rows, rows), 0) + i * step_rows
        pick_a = jnp.where(place == target_a, count, 0.0).astype(BF16)
        pick_b = jnp.where((place & -5) == target_b, count, 0.0).astype(BF16)
        vis = vis_ref[...]
        got_a = dot(pick_a, vis)
        got_b = dot(pick_b, vis)
        low = (iota((step_rows, 128), 0) & 4) == 0
        mixed = jnp.where(low, got_b[:, :128], got_b[:, 128:])
        at = pl.ds(i * step_owners, step_owners)
        send[at, 0] = got_a[:, :128].reshape(step_owners, 8, 128).astype(BF16)
        send[at, 1] = got_a[:, 128:].reshape(step_owners, 8, 128).astype(BF16)
        send[at, 2] = mixed.reshape(step_owners, 8, 128).astype(BF16)
        return carry

    lax.fori_loop(0, n // step_owners, pack, 0)

    pl.semaphore_wait(barrier, n - 1 + nchan - 1)

    def send_meta(pair):
        pltpu.make_async_remote_copy(
            meta_send.at[pair], meta_recv.at[me], meta_s, meta_r,
            device_id={"chan": chan, "pair": pair}, device_id_type=MESH).start()

    groups = chips // nchan
    group = lax.div(chip, nchan)
    keeper = lax.rem(chip, nchan) == chan

    def send_metas(i, carry):
        peer = lax.rem(group + i, groups) * nchan + chan
        send_meta(peer * 2)
        send_meta(peer * 2 + 1)
        return carry

    lax.fori_loop(1, groups, send_metas, 0)

    @pl.when(keeper)
    def _():
        send_meta(chip * 2 + 1 - core)
        pltpu.make_async_copy(meta_send.at[me], meta_recv.at[me], meta_r).start()

    @pl.when(jnp.logical_not(keeper))
    def _():
        send_meta((group * nchan + chan) * 2)
        send_meta((group * nchan + chan) * 2 + 1)

    own_data = pltpu.make_async_copy(send.at[me], recv.at[me], data_r)
    own_data.start()

    def ship(peer):
        pltpu.make_async_remote_copy(
            send.at[peer], recv.at[me], data_s, data_r,
            device_id={"chan": chan, "pair": peer}, device_id_type=MESH).start()

    def ship_chip(peer):
        ship(peer * 2 + core)
        ship(peer * 2 + 1 - core)

    each_chip(ship_chip)
    ship(chip * 2 + 1 - core)

    beam_copy.wait()
    mwin, modes = beam_buf.shape[0], beam_buf.shape[3]
    base = beam_buf.shape[2]
    width = min(128, modes)
    turned = width // 2
    for m in range(mwin):
        for r in range(2):
            def turn(i, carry, m=m, r=r):
                at = pl.ds(pl.multiple_of(i * width, width), width)
                full = jnp.transpose(beam_buf[m, r, :, at])
                high = full.astype(BF16).astype(F32)
                low = full - high
                high, low = high.reshape(width // 16, 2, 8, base), low.reshape(width // 16, 2, 8, base)
                to = pl.ds(pl.multiple_of(i * turned, turned), turned)
                for half in range(2):
                    beam_t[m, half, to, r * base:(r + 1) * base] = high[:, half].reshape(turned, base).astype(BF16)
                    beam_t[m, half, to, (2 + r) * base:(3 + r) * base] = low[:, half].reshape(turned, base).astype(BF16)
                return carry

            lax.fori_loop(0, modes // width, turn, 0)

    right[:, 2 * base:, 128:] = jnp.zeros((mwin, 2 * base, 128), BF16)

    @pl.when(keeper)
    def _():
        pltpu.make_async_copy(meta_recv, meta_recv, meta_r).wait()
        for i in range(1, nchan):
            pltpu.make_async_remote_copy(
                meta_recv, meta_recv, hand_s.at[i], hand_r,
                device_id={"chan": lax.rem(chan + i, nchan), "pair": me}, device_id_type=MESH).start()

    @pl.when(jnp.logical_not(keeper))
    def _():
        pltpu.make_async_copy(meta_recv, meta_recv, hand_r).wait()

    code = jnp.transpose(meta_recv[...].reshape(n, 128))[:16]
    weight = jnp.floor(code * (1.0 / 128.0))
    place = code - weight * 128.0
    both = jnp.concatenate([place, weight], axis=0).astype(BF16)
    spread = dot(both, jnp.where(iota((n, n * 8), 0) == iota((n, n * 8), 1) // 8, 1.0, 0.0).astype(BF16))
    ranks = iota((16, n * 8), 0)
    in_message = iota((16, n * 8), 1) & 7
    at_a = ranks == in_message
    at_b = ranks == 8 + (in_message & 3)

    def flat(values, mask):
        return jnp.sum(jnp.where(mask, values, 0.0), axis=0, keepdims=True)

    slot_a, slot_b = flat(spread[:16], at_a), flat(spread[:16], at_b)
    weight_a, weight_b = flat(spread[16:], at_a), flat(spread[16:], at_b)
    bases = iota((base, n * 8), 0).astype(F32)
    first = (iota((base, n * 8), 1) & 4) == 0
    hit_a = jnp.where(bases == slot_a, 1.0, 0.0)
    hit_b = jnp.where(bases == slot_b, 1.0, 0.0)
    hot_a[...] = hit_a.astype(BF16)
    hot_b[:base] = jnp.where(first, hit_b, 0.0).astype(BF16)
    hot_b[base:] = jnp.where(first, 0.0, hit_b).astype(BF16)
    denom = jnp.sum(hit_a * weight_a + jnp.where(first, hit_b, 0.0) * weight_b, axis=1, keepdims=True)
    bottom[...] = jnp.broadcast_to(jnp.maximum(denom, 1.0), (base, 128))

    pltpu.make_async_copy(recv, recv, data_r).wait()

    early = jnp.concatenate([recv[:, 0].reshape(n * 8, 128), recv[:, 1].reshape(n * 8, 128)], axis=1)
    numer = dot(hot_a[...], early)
    late = dot(hot_b[...], recv[:, 2].reshape(n * 8, 128))
    numer = (numer[:, :128] + late[:base], numer[:, 128:] + late[base:])
    sign = jnp.where(iota((base, 128), 1) < sets, 1.0, -1.0)
    for m in range(mwin):
        stacked = numer[m] / bottom[...]
        swapped = jnp.concatenate([stacked[:, sets:], stacked[:, :sets]], axis=1) * sign
        for r, half in enumerate((stacked, swapped)):
            high = half.astype(BF16)
            right[m, r * base:(r + 1) * base, :128] = high
            right[m, (2 + r) * base:(3 + r) * base, :128] = high
            right[m, r * base:(r + 1) * base, 128:] = (half - high.astype(F32)).astype(BF16)

    step_modes = min(256, modes // 2)
    step_blocks = step_modes // 8

    pieces = modes // 2 // step_modes

    def project(parity, to, m, i):
        both = dot(beam_t[m, parity, i * step_modes:(i + 1) * step_modes, :], right[m])
        sums = both[:, :128] + both[:, 128:]
        part[to, m, i * step_blocks:(i + 1) * step_blocks] = sums.reshape(step_blocks, 8, 128)

    to_core = []
    for m in range(mwin):
        for i in range(pieces):
            project(1 - core, 0, m, i)
            at = pl.ds(i * step_blocks, step_blocks)
            to_core.append(pltpu.make_async_remote_copy(
                part.at[0, m, at], core_recv.at[m, at], core_s.at[m, i], core_r.at[m, i],
                device_id={"chan": chan, "pair": chip * 2 + 1 - core}, device_id_type=MESH))
            to_core[-1].start()
    for m in range(mwin):
        for i in range(pieces):
            project(core, 1, m, i)

    top = jnp.zeros((8, 128), F32)
    step_chips = min(8, step_blocks)
    for m in range(mwin):
        for i in range(pieces):
            to_core[m * pieces + i].wait_recv()

            def merge(j, top, m=m, i=i):
                at = pl.ds(i * step_blocks + j * step_chips, step_chips)
                sums = part[1, m, at] + core_recv[m, at]
                part[1, m, at] = sums
                return jnp.maximum(top, jnp.max(jnp.abs(sums), axis=0))

            top = lax.fori_loop(0, step_blocks // step_chips, merge, top)
    peak = jnp.max(jnp.max(top, axis=1, keepdims=True), axis=0, keepdims=True)
    peak = jnp.maximum(peak, 1e-30)
    scale_send[...] = jnp.broadcast_to(peak * (1.0 / 32000.0), (1, 128))
    factor = jnp.broadcast_to(32000.0 / peak, (8, 128))

    def code_sums(i, carry):
        at = pl.ds(i * step_chips, step_chips)
        scaled = jnp.concatenate([part[1, 0, at] * factor, part[1, 1, at] * factor], axis=2)
        send2[at] = jnp.round(scaled).astype(I32).astype(I16)
        return carry

    lax.fori_loop(0, chips // step_chips, code_sums, 0)

    own_scale = pltpu.make_async_copy(scale_send, scale_recv.at[chip], scale_r)
    own_scale.start()
    own_red = pltpu.make_async_copy(send2.at[chip], recv2.at[chip], red_r)
    own_red.start()

    def send_red(peer):
        target = {"chan": chan, "pair": peer * 2 + core}
        pltpu.make_async_remote_copy(
            send2.at[peer], recv2.at[chip], red_s, red_r, device_id=target, device_id_type=MESH).start()
        pltpu.make_async_remote_copy(
            scale_send, scale_recv.at[chip], scale_s, scale_r, device_id=target, device_id_type=MESH).start()

    each_chip(send_red)
    pltpu.make_async_copy(scale_recv, scale_recv, scale_r).wait()
    pltpu.make_async_copy(recv2, recv2, red_r).wait()

    step_adds = min(8, chips)

    def add_up(i, sums):
        for j in range(step_adds):
            scale = scale_recv[i * step_adds + j]
            sums = sums + recv2[i * step_adds + j].astype(I32).astype(F32) * jnp.concatenate([scale, scale], axis=1)
        return sums

    total = lax.fori_loop(0, chips // step_adds, add_up, jnp.zeros((8, columns), F32))
    total_buf[...] = total
    modes_out = pltpu.make_async_copy(total_buf, result_hbm, out_sem)
    modes_out.start()
    square = total * total
    power_0 = jnp.sum(square[:, :128], axis=1, keepdims=True)
    power_1 = jnp.sum(square[:, 128:], axis=1, keepdims=True)
    pow_send[...] = jnp.where(iota((8, 128), 1) == 0, power_0, power_1)
    own_power = pltpu.make_async_copy(pow_send, power_hbm.at[chan], own_sem)
    own_power.start()
    sends = []
    for i in range(1, nchan):
        peer = lax.rem(chan + i, nchan)
        copy = pltpu.make_async_remote_copy(
            pow_send, power_hbm.at[chan], pow_s.at[i], pow_r.at[i],
            device_id={"chan": peer, "pair": me}, device_id_type=MESH)
        copy.start()
        sends.append(copy)
    for copy in sends:
        copy.wait()
    own_power.wait()
    modes_out.wait()

    for copy in to_core:
        copy.wait_send()
    sent = 2 * groups

    @pl.when(keeper)
    def _():
        pltpu.make_async_copy(meta_send.at[pl.ds(0, sent - 1)], meta_send.at[pl.ds(0, sent - 1)], meta_s).wait()
        for i in range(1, nchan):
            pltpu.make_async_copy(meta_recv, meta_recv, hand_s.at[i]).wait()

    @pl.when(jnp.logical_not(keeper))
    def _():
        pltpu.make_async_copy(meta_send.at[pl.ds(0, sent)], meta_send.at[pl.ds(0, sent)], meta_s).wait()

    pltpu.make_async_copy(send.at[pl.ds(1, n - 1)], send.at[pl.ds(1, n - 1)], data_s).wait()
    pltpu.make_async_copy(send2.at[pl.ds(1, chips - 1)], send2.at[pl.ds(1, chips - 1)], red_s).wait()
    pltpu.make_async_copy(scale_recv.at[pl.ds(1, chips - 1)], scale_recv.at[pl.ds(1, chips - 1)], scale_s).wait()


def shape_results(mwin, sets, result_ref, powers_ref, modes_ref, power_ref):
    for m in range(mwin):
        for part in range(2):
            at = (2 * m + part) * sets
            modes_ref[:, m, part, :] = result_ref[:, at:at + sets]
    power = jnp.sum(powers_ref[...], axis=0) * (1.0 / (powers_ref.shape[0] * sets))
    power_ref[...] = jnp.transpose(power)[:mwin]


def per_device(visibility, pair_counts, owner_ids, slot_ids, beam):
    n, nchan = lax.axis_size("pair"), lax.axis_size("chan")
    rows, columns = visibility.shape[1:]
    mwin, _, base, modes = beam.shape[1:]
    sets = columns // (2 * mwin)
    chips = n // 2
    vmem, hbm = pl.BlockSpec(memory_space=pltpu.VMEM), pl.BlockSpec(memory_space=pltpu.HBM)
    dma = pltpu.SemaphoreType.DMA
    amplitudes, powers = pl.pallas_call(
        functools.partial(body, n, nchan, sets),
        out_shape=(
            jax.ShapeDtypeStruct((8, columns), F32),
            jax.ShapeDtypeStruct((nchan, 8, 128), F32),
        ),
        in_specs=[hbm] * 5,
        out_specs=(hbm, hbm),
        scratch_shapes=[
            pltpu.VMEM((1, rows), I32),
            pltpu.VMEM((1, rows), I32),
            pltpu.VMEM((1, rows), I32),
            pltpu.VMEM((rows, columns), BF16),
            pltpu.VMEM((n, 3, 8, 128), BF16),
            pltpu.VMEM((n, 3, 8, 128), BF16),
            pltpu.VMEM((n, 1, 128), F32),
            pltpu.VMEM((n, 1, 128), F32),
            pltpu.VMEM((mwin, 2, base, modes), F32),
            pltpu.VMEM((mwin, 2, modes // 2, 4 * base), BF16),
            pltpu.VMEM((base, n * 8), BF16),
            pltpu.VMEM((2 * base, n * 8), BF16),
            pltpu.VMEM((base, 128), F32),
            pltpu.VMEM((mwin, 4 * base, 256), BF16),
            pltpu.VMEM((2, mwin, chips, 8, 128), F32),
            pltpu.VMEM((mwin, chips, 8, 128), F32),
            pltpu.VMEM((chips, 8, columns), I16),
            pltpu.VMEM((chips, 8, columns), I16),
            pltpu.VMEM((1, 128), F32),
            pltpu.VMEM((chips, 1, 128), F32),
            pltpu.VMEM((8, columns), F32),
            pltpu.VMEM((8, 128), F32),
            dma((4,)), dma, dma, dma, dma((nchan,)), dma, dma, dma, dma((mwin, 2)), dma((mwin, 2)), dma, dma, dma, dma,
            dma((nchan,)), dma((nchan,)), dma, dma,
        ],
        compiler_params=pltpu.CompilerParams(
            collective_id=0, has_side_effects=True
        ),
        name="stack_project",
    )(
        owner_ids.reshape(1, rows), slot_ids.reshape(1, rows), pair_counts.reshape(1, rows),
        visibility[0], beam[0],
    )
    shaped, power = pl.pallas_call(
        functools.partial(shape_results, mwin, sets),
        out_shape=(jax.ShapeDtypeStruct((8, mwin, 2, sets), F32), jax.ShapeDtypeStruct((mwin, 8), F32)),
        in_specs=[vmem] * 2,
        out_specs=(vmem, vmem),
        name="shape_results",
    )(amplitudes, powers)
    return shaped[None], power.T


def solution(mesh):
    in_specs = (
        P("chan", "pair", None),
        P("pair"),
        P("pair", None),
        P("pair"),
        P("chan", None, None, "pair", None),
    )
    out_specs = (P("chan", "pair", None, None, None), P("pair", None))
    return jax.shard_map(
        per_device, mesh=mesh, in_specs=in_specs, out_specs=out_specs, check_vma=False
    )
```

```python
import functools

import jax
import jax.numpy as jnp
from jax import lax
from jax.experimental import pallas as pl
from jax.experimental.pallas import tpu as pltpu
from jax.sharding import PartitionSpec as P

MESH = pl.DeviceIdType.MESH
F32, BF16, I32, I16 = jnp.float32, jnp.bfloat16, jnp.int32, jnp.int16


def iota(shape, axis):
    return lax.broadcasted_iota(I32, shape, axis)


def dot(a, b):
    return jnp.dot(a, b, preferred_element_type=F32)


def dot_nt(a, b):
    return lax.dot_general(a, b, (((1,), (1,)), ((), ())), preferred_element_type=F32)


def body(
    n, nchan, sets,
    owner_hbm, slot_hbm, count_hbm, vis_hbm, beam_hbm,
    result_hbm, power_hbm,
    owner_ref, slot_ref, count_ref, vis_ref,
    send, recv, meta_send, meta_recv,
    beam_buf, beam_t, hot_a, hot_b, bottom, right,
    part, core_recv, send2, recv2, scale_send, scale_recv, total_buf, pow_send,
    in_sem, beam_sem, meta_s, meta_r, hand_s, hand_r, data_s, data_r, core_s, core_r, red_s, red_r, scale_s, scale_r, pow_s, pow_r, out_sem, own_sem,
):
    chan = lax.axis_index("chan")
    me = lax.axis_index("pair")
    chips = n // 2
    chip, core = me // 2, me % 2
    rows, columns = vis_ref.shape
    step_chips = min(8, chips)

    loads = [
        pltpu.make_async_copy(src, dst, in_sem.at[i])
        for i, (src, dst) in enumerate((
            (owner_hbm, owner_ref), (slot_hbm, slot_ref), (count_hbm, count_ref), (vis_hbm, vis_ref),
        ))
    ]
    for load in loads:
        load.start()
    beam_copy = pltpu.make_async_copy(beam_hbm, beam_buf, beam_sem)
    beam_copy.start()

    barrier = pltpu.get_barrier_semaphore()

    side = 8
    while side * side > chips:
        side //= 2
    depth = chips // side
    chip_row, chip_spot = lax.div(chip, side), lax.rem(chip, side)

    turn_sign = 1 - 2 * core

    def far(k, size):
        half = lax.div(k, 2) if not isinstance(k, int) else k // 2
        return size // 2 + turn_sign * (half - (k - 2 * half) * (2 * half + 1))

    def own_row(visit):
        for k in range(side - 1):
            visit(chip_row * side + lax.rem(chip_spot + far(k, side), side))

    def other_rows(visit):
        def diagonal(total, carry):
            def step(k, carry):
                line = lax.rem(chip_row + far(k, depth), depth)
                visit(line * side + lax.rem(chip_spot + far(total - k, side), side))
                return carry

            return lax.fori_loop(lax.max(0, total - side + 1), lax.min(depth - 1, total + 1), step, carry)

        lax.fori_loop(0, depth + side - 2, diagonal, 0)

    def each_chip(visit):
        own_row(visit)
        other_rows(visit)

    def greet(pair):
        pl.semaphore_signal(barrier, inc=1, device_id={"chan": chan, "pair": pair}, device_id_type=MESH)

    def greet_chip(peer):
        greet(peer * 2)
        greet(peer * 2 + 1)

    other_rows(greet_chip)
    own_row(greet_chip)
    greet(chip * 2 + 1 - core)
    for i in range(1, nchan):
        peer = lax.rem(chan + i, nchan)
        pl.semaphore_signal(barrier, inc=1, device_id={"chan": peer, "pair": me}, device_id_type=MESH)

    for load in loads:
        load.wait()

    owner = owner_ref[...]
    count = count_ref[...].astype(F32)
    slot = slot_ref[...].astype(F32)
    own_hot = jnp.where(iota((n, rows), 0) == owner, 1.0, 0.0).astype(BF16)
    before = jnp.where(iota((rows, rows), 0) < iota((rows, rows), 1), 1.0, 0.0).astype(BF16)
    rank = jnp.sum(own_hot.astype(F32) * dot(own_hot, before), axis=0, keepdims=True).astype(I32)

    lane_hit = iota((128, rows), 0) == rank
    by_slot = jnp.where(lane_hit, slot, 0.0).astype(BF16)
    by_count = jnp.where(lane_hit, count * 128.0, 0.0).astype(BF16)
    meta = dot_nt(own_hot, by_slot) + dot_nt(own_hot, by_count)
    meta_send[...] = meta.reshape(n, 1, 128)

    target_a = jnp.where(rank < 8, owner * 8 + rank, -1)
    target_b = jnp.where(rank >= 8, owner * 8 + rank - 8, -1)
    step_owners = min(16, n)
    step_rows = step_owners * 8

    def pack(i, carry):
        place = iota((step_rows, rows), 0) + i * step_rows
        pick_a = jnp.where(place == target_a, count, 0.0).astype(BF16)
        pick_b = jnp.where((place & -5) == target_b, count, 0.0).astype(BF16)
        vis = vis_ref[...]
        got_a = dot(pick_a, vis)
        got_b = dot(pick_b, vis)
        low = (iota((step_rows, 128), 0) & 4) == 0
        mixed = jnp.where(low, got_b[:, :128], got_b[:, 128:])
        at = pl.ds(i * step_owners, step_owners)
        send[at, 0] = got_a[:, :128].reshape(step_owners, 8, 128).astype(BF16)
        send[at, 1] = got_a[:, 128:].reshape(step_owners, 8, 128).astype(BF16)
        send[at, 2] = mixed.reshape(step_owners, 8, 128).astype(BF16)
        return carry

    lax.fori_loop(0, n // step_owners, pack, 0)

    pl.semaphore_wait(barrier, n - 1 + nchan - 1)

    def send_meta(pair):
        pltpu.make_async_remote_copy(
            meta_send.at[pair], meta_recv.at[me], meta_s, meta_r,
            device_id={"chan": chan, "pair": pair}, device_id_type=MESH).start()

    groups = chips // nchan
    group = lax.div(chip, nchan)
    keeper = lax.rem(chip, nchan) == chan

    def send_metas(i, carry):
        peer = lax.rem(group + i, groups) * nchan + chan
        send_meta(peer * 2)
        send_meta(peer * 2 + 1)
        return carry

    lax.fori_loop(1, groups, send_metas, 0)

    @pl.when(keeper)
    def _():
        send_meta(chip * 2 + 1 - core)
        pltpu.make_async_copy(meta_send.at[me], meta_recv.at[me], meta_r).start()

    @pl.when(jnp.logical_not(keeper))
    def _():
        send_meta((group * nchan + chan) * 2)
        send_meta((group * nchan + chan) * 2 + 1)

    own_data = pltpu.make_async_copy(send.at[me], recv.at[me], data_r)
    own_data.start()

    def ship(peer):
        pltpu.make_async_remote_copy(
            send.at[peer], recv.at[me], data_s, data_r,
            device_id={"chan": chan, "pair": peer}, device_id_type=MESH).start()

    def ship_chip(peer):
        ship(peer * 2 + core)
        ship(peer * 2 + 1 - core)

    each_chip(ship_chip)
    ship(chip * 2 + 1 - core)

    beam_copy.wait()
    mwin, modes = beam_buf.shape[0], beam_buf.shape[3]
    base = beam_buf.shape[2]
    width = min(128, modes)
    turned = width // 2
    for m in range(mwin):
        for r in range(2):
            def turn(i, carry, m=m, r=r):
                at = pl.ds(pl.multiple_of(i * width, width), width)
                full = jnp.transpose(beam_buf[m, r, :, at])
                high = full.astype(BF16).astype(F32)
                low = full - high
                high, low = high.reshape(width // 16, 2, 8, base), low.reshape(width // 16, 2, 8, base)
                to = pl.ds(pl.multiple_of(i * turned, turned), turned)
                for half in range(2):
                    beam_t[m, half, to, r * base:(r + 1) * base] = high[:, half].reshape(turned, base).astype(BF16)
                    beam_t[m, half, to, (2 + r) * base:(3 + r) * base] = low[:, half].reshape(turned, base).astype(BF16)
                return carry

            lax.fori_loop(0, modes // width, turn, 0)

    right[:, 2 * base:, 128:] = jnp.zeros((mwin, 2 * base, 128), BF16)

    @pl.when(keeper)
    def _():
        pltpu.make_async_copy(meta_recv, meta_recv, meta_r).wait()
        for i in range(1, nchan):
            pltpu.make_async_remote_copy(
                meta_recv, meta_recv, hand_s.at[i], hand_r,
                device_id={"chan": lax.rem(chan + i, nchan), "pair": me}, device_id_type=MESH).start()

    @pl.when(jnp.logical_not(keeper))
    def _():
        pltpu.make_async_copy(meta_recv, meta_recv, hand_r).wait()

    code = jnp.transpose(meta_recv[...].reshape(n, 128))[:16]
    weight = jnp.floor(code * (1.0 / 128.0))
    place = code - weight * 128.0
    both = jnp.concatenate([place, weight], axis=0).astype(BF16)
    spread = dot(both, jnp.where(iota((n, n * 8), 0) == iota((n, n * 8), 1) // 8, 1.0, 0.0).astype(BF16))
    ranks = iota((16, n * 8), 0)
    in_message = iota((16, n * 8), 1) & 7
    at_a = ranks == in_message
    at_b = ranks == 8 + (in_message & 3)

    def flat(values, mask):
        return jnp.sum(jnp.where(mask, values, 0.0), axis=0, keepdims=True)

    slot_a, slot_b = flat(spread[:16], at_a), flat(spread[:16], at_b)
    weight_a, weight_b = flat(spread[16:], at_a), flat(spread[16:], at_b)
    first = (iota((16, n * 8), 1) & 4) == 0

    def mark(i, carry):
        at = pl.multiple_of(i * 16, 16)
        bases = (iota((16, n * 8), 0) + at).astype(F32)
        hit_a = jnp.where(bases == slot_a, 1.0, 0.0)
        hit_b = jnp.where(bases == slot_b, 1.0, 0.0)
        hit_0 = jnp.where(first, hit_b, 0.0)
        hot_a[pl.ds(at, 16)] = hit_a.astype(BF16)
        hot_b[pl.ds(at, 16)] = hit_0.astype(BF16)
        hot_b[pl.ds(base + at, 16)] = (hit_b - hit_0).astype(BF16)
        denom = jnp.sum(hit_a * weight_a + hit_0 * weight_b, axis=1, keepdims=True)
        bottom[pl.ds(at, 16)] = jnp.broadcast_to(jnp.maximum(denom, 1.0), (16, 128))
        return carry

    lax.fori_loop(0, base // 16, mark, 0)

    pltpu.make_async_copy(recv, recv, data_r).wait()

    early = jnp.concatenate([recv[:, 0].reshape(n * 8, 128), recv[:, 1].reshape(n * 8, 128)], axis=1)
    numer = dot(hot_a[...], early)
    late = dot(hot_b[...], recv[:, 2].reshape(n * 8, 128))
    numer = (numer[:, :128] + late[:base], numer[:, 128:] + late[base:])
    sign = jnp.where(iota((base, 128), 1) < sets, 1.0, -1.0)
    for m in range(mwin):
        stacked = numer[m] / bottom[...]
        swapped = jnp.concatenate([stacked[:, sets:], stacked[:, :sets]], axis=1) * sign
        for r, half in enumerate((stacked, swapped)):
            high = half.astype(BF16)
            right[m, r * base:(r + 1) * base, :128] = high
            right[m, (2 + r) * base:(3 + r) * base, :128] = high
            right[m, r * base:(r + 1) * base, 128:] = (half - high.astype(F32)).astype(BF16)

    step_modes = min(256, modes // 2)
    step_blocks = step_modes // 8

    pieces = modes // 2 // step_modes

    def project(parity, to, m, i):
        both = dot(beam_t[m, parity, i * step_modes:(i + 1) * step_modes, :], right[m])
        sums = both[:, :128] + both[:, 128:]
        part[to, m, i * step_blocks:(i + 1) * step_blocks] = sums.reshape(step_blocks, 8, 128)

    to_core = []
    for m in range(mwin):
        for i in range(pieces):
            project(1 - core, 0, m, i)
            at = pl.ds(i * step_blocks, step_blocks)
            to_core.append(pltpu.make_async_remote_copy(
                part.at[0, m, at], core_recv.at[m, at], core_s.at[m, i], core_r.at[m, i],
                device_id={"chan": chan, "pair": chip * 2 + 1 - core}, device_id_type=MESH))
            to_core[-1].start()
    for m in range(mwin):
        for i in range(pieces):
            project(core, 1, m, i)

    top = jnp.zeros((8, 128), F32)
    step_chips = min(8, step_blocks)
    for m in range(mwin):
        for i in range(pieces):
            to_core[m * pieces + i].wait_recv()

            def merge(j, top, m=m, i=i):
                at = pl.ds(i * step_blocks + j * step_chips, step_chips)
                sums = part[1, m, at] + core_recv[m, at]
                part[1, m, at] = sums
                return jnp.maximum(top, jnp.max(jnp.abs(sums), axis=0))

            top = lax.fori_loop(0, step_blocks // step_chips, merge, top)
    peak = jnp.max(jnp.max(top, axis=1, keepdims=True), axis=0, keepdims=True)
    peak = jnp.maximum(peak, 1e-30)
    scale_send[...] = jnp.broadcast_to(peak * (1.0 / 32000.0), (1, 128))
    factor = jnp.broadcast_to(32000.0 / peak, (8, 128))

    def code_sums(i, carry):
        at = pl.ds(i * step_chips, step_chips)
        scaled = jnp.concatenate([part[1, 0, at] * factor, part[1, 1, at] * factor], axis=2)
        send2[at] = jnp.round(scaled).astype(I32).astype(I16)
        return carry

    lax.fori_loop(0, chips // step_chips, code_sums, 0)

    own_scale = pltpu.make_async_copy(scale_send, scale_recv.at[chip], scale_r)
    own_scale.start()
    own_red = pltpu.make_async_copy(send2.at[chip], recv2.at[chip], red_r)
    own_red.start()

    def send_red(peer):
        target = {"chan": chan, "pair": peer * 2 + core}
        pltpu.make_async_remote_copy(
            send2.at[peer], recv2.at[chip], red_s, red_r, device_id=target, device_id_type=MESH).start()
        pltpu.make_async_remote_copy(
            scale_send, scale_recv.at[chip], scale_s, scale_r, device_id=target, device_id_type=MESH).start()

    each_chip(send_red)
    pltpu.make_async_copy(scale_recv, scale_recv, scale_r).wait()
    pltpu.make_async_copy(recv2, recv2, red_r).wait()

    step_adds = min(8, chips)

    def add_up(i, sums):
        for j in range(step_adds):
            scale = scale_recv[i * step_adds + j]
            sums = sums + recv2[i * step_adds + j].astype(I32).astype(F32) * jnp.concatenate([scale, scale], axis=1)
        return sums

    total = lax.fori_loop(0, chips // step_adds, add_up, jnp.zeros((8, columns), F32))
    total_buf[...] = total
    modes_out = pltpu.make_async_copy(total_buf, result_hbm, out_sem)
    modes_out.start()
    square = total * total
    power_0 = jnp.sum(square[:, :128], axis=1, keepdims=True)
    power_1 = jnp.sum(square[:, 128:], axis=1, keepdims=True)
    pow_send[...] = jnp.where(iota((8, 128), 1) == 0, power_0, power_1)
    own_power = pltpu.make_async_copy(pow_send, power_hbm.at[chan], own_sem)
    own_power.start()
    sends = []
    for i in range(1, nchan):
        peer = lax.rem(chan + i, nchan)
        copy = pltpu.make_async_remote_copy(
            pow_send, power_hbm.at[chan], pow_s.at[i], pow_r.at[i],
            device_id={"chan": peer, "pair": me}, device_id_type=MESH)
        copy.start()
        sends.append(copy)
    for copy in sends:
        copy.wait()
    own_power.wait()
    modes_out.wait()

    for copy in to_core:
        copy.wait_send()
    sent = 2 * groups

    @pl.when(keeper)
    def _():
        pltpu.make_async_copy(meta_send.at[pl.ds(0, sent - 1)], meta_send.at[pl.ds(0, sent - 1)], meta_s).wait()
        for i in range(1, nchan):
            pltpu.make_async_copy(meta_recv, meta_recv, hand_s.at[i]).wait()

    @pl.when(jnp.logical_not(keeper))
    def _():
        pltpu.make_async_copy(meta_send.at[pl.ds(0, sent)], meta_send.at[pl.ds(0, sent)], meta_s).wait()

    pltpu.make_async_copy(send.at[pl.ds(1, n - 1)], send.at[pl.ds(1, n - 1)], data_s).wait()
    pltpu.make_async_copy(send2.at[pl.ds(1, chips - 1)], send2.at[pl.ds(1, chips - 1)], red_s).wait()
    pltpu.make_async_copy(scale_recv.at[pl.ds(1, chips - 1)], scale_recv.at[pl.ds(1, chips - 1)], scale_s).wait()


def shape_results(mwin, sets, result_ref, powers_ref, modes_ref, power_ref):
    for m in range(mwin):
        for part in range(2):
            at = (2 * m + part) * sets
            modes_ref[:, m, part, :] = result_ref[:, at:at + sets]
    power = jnp.sum(powers_ref[...], axis=0) * (1.0 / (powers_ref.shape[0] * sets))
    power_ref[...] = jnp.transpose(power)[:mwin]


def per_device(visibility, pair_counts, owner_ids, slot_ids, beam):
    n, nchan = lax.axis_size("pair"), lax.axis_size("chan")
    rows, columns = visibility.shape[1:]
    mwin, _, base, modes = beam.shape[1:]
    sets = columns // (2 * mwin)
    chips = n // 2
    vmem, hbm = pl.BlockSpec(memory_space=pltpu.VMEM), pl.BlockSpec(memory_space=pltpu.HBM)
    dma = pltpu.SemaphoreType.DMA
    amplitudes, powers = pl.pallas_call(
        functools.partial(body, n, nchan, sets),
        out_shape=(
            jax.ShapeDtypeStruct((8, columns), F32),
            jax.ShapeDtypeStruct((nchan, 8, 128), F32),
        ),
        in_specs=[hbm] * 5,
        out_specs=(hbm, hbm),
        scratch_shapes=[
            pltpu.VMEM((1, rows), I32),
            pltpu.VMEM((1, rows), I32),
            pltpu.VMEM((1, rows), I32),
            pltpu.VMEM((rows, columns), BF16),
            pltpu.VMEM((n, 3, 8, 128), BF16),
            pltpu.VMEM((n, 3, 8, 128), BF16),
            pltpu.VMEM((n, 1, 128), F32),
            pltpu.VMEM((n, 1, 128), F32),
            pltpu.VMEM((mwin, 2, base, modes), F32),
            pltpu.VMEM((mwin, 2, modes // 2, 4 * base), BF16),
            pltpu.VMEM((base, n * 8), BF16),
            pltpu.VMEM((2 * base, n * 8), BF16),
            pltpu.VMEM((base, 128), F32),
            pltpu.VMEM((mwin, 4 * base, 256), BF16),
            pltpu.VMEM((2, mwin, chips, 8, 128), F32),
            pltpu.VMEM((mwin, chips, 8, 128), F32),
            pltpu.VMEM((chips, 8, columns), I16),
            pltpu.VMEM((chips, 8, columns), I16),
            pltpu.VMEM((1, 128), F32),
            pltpu.VMEM((chips, 1, 128), F32),
            pltpu.VMEM((8, columns), F32),
            pltpu.VMEM((8, 128), F32),
            dma((4,)), dma, dma, dma, dma((nchan,)), dma, dma, dma, dma((mwin, 2)), dma((mwin, 2)), dma, dma, dma, dma,
            dma((nchan,)), dma((nchan,)), dma, dma,
        ],
        compiler_params=pltpu.CompilerParams(
            collective_id=0, has_side_effects=True
        ),
        name="stack_project",
    )(
        owner_ids.reshape(1, rows), slot_ids.reshape(1, rows), pair_counts.reshape(1, rows),
        visibility[0], beam[0],
    )
    shaped, power = pl.pallas_call(
        functools.partial(shape_results, mwin, sets),
        out_shape=(jax.ShapeDtypeStruct((8, mwin, 2, sets), F32), jax.ShapeDtypeStruct((mwin, 8), F32)),
        in_specs=[vmem] * 2,
        out_specs=(vmem, vmem),
        name="shape_results",
    )(amplitudes, powers)
    return shaped[None], power.T


def solution(mesh):
    in_specs = (
        P("chan", "pair", None),
        P("pair"),
        P("pair", None),
        P("pair"),
        P("chan", None, None, "pair", None),
    )
    out_specs = (P("chan", "pair", None, None, None), P("pair", None))
    return jax.shard_map(
        per_device, mesh=mesh, in_specs=in_specs, out_specs=out_specs, check_vma=False
    )
```

```python
import functools

import jax
import jax.numpy as jnp
from jax import lax
from jax.experimental import pallas as pl
from jax.experimental.pallas import tpu as pltpu
from jax.sharding import PartitionSpec as P

MESH = pl.DeviceIdType.MESH
F32, BF16, I32, I16 = jnp.float32, jnp.bfloat16, jnp.int32, jnp.int16


def iota(shape, axis):
    return lax.broadcasted_iota(I32, shape, axis)


def dot(a, b):
    return jnp.dot(a, b, preferred_element_type=F32)


def dot_nt(a, b):
    return lax.dot_general(a, b, (((1,), (1,)), ((), ())), preferred_element_type=F32)


def body(
    n, nchan, sets,
    owner_hbm, slot_hbm, count_hbm, vis_hbm, beam_hbm,
    result_hbm, power_hbm,
    owner_ref, slot_ref, count_ref, vis_ref,
    send, recv, meta_send, meta_recv,
    beam_buf, beam_t, hot_a, hot_b, bottom, right,
    part, core_recv, send2, recv2, scale_send, scale_recv, total_buf, pow_send,
    in_sem, beam_sem, meta_s, meta_r, hand_s, hand_r, data_s, data_r, core_s, core_r, red_s, red_r, scale_s, scale_r, pow_s, pow_r, out_sem, own_sem,
):
    chan = lax.axis_index("chan")
    me = lax.axis_index("pair")
    chips = n // 2
    chip, core = me // 2, me % 2
    rows, columns = vis_ref.shape
    step_chips = min(8, chips)

    loads = [
        pltpu.make_async_copy(src, dst, in_sem.at[i])
        for i, (src, dst) in enumerate((
            (owner_hbm, owner_ref), (slot_hbm, slot_ref), (count_hbm, count_ref), (vis_hbm, vis_ref),
        ))
    ]
    for load in loads:
        load.start()
    beam_copy = pltpu.make_async_copy(beam_hbm, beam_buf, beam_sem)
    beam_copy.start()

    barrier = pltpu.get_barrier_semaphore()

    side = 8
    while side * side > chips:
        side //= 2
    depth = chips // side
    chip_row, chip_spot = lax.div(chip, side), lax.rem(chip, side)

    turn_sign = 1 - 2 * core

    def far(k, size):
        half = lax.div(k, 2) if not isinstance(k, int) else k // 2
        return size // 2 + turn_sign * (half - (k - 2 * half) * (2 * half + 1))

    def own_row(visit):
        for k in range(side - 1):
            visit(chip_row * side + lax.rem(chip_spot + far(k, side), side))

    def other_rows(visit):
        def diagonal(total, carry):
            def step(k, carry):
                line = lax.rem(chip_row + far(k, depth), depth)
                visit(line * side + lax.rem(chip_spot + far(total - k, side), side))
                return carry

            return lax.fori_loop(lax.max(0, total - side + 1), lax.min(depth - 1, total + 1), step, carry)

        lax.fori_loop(0, depth + side - 2, diagonal, 0)

    def greet(pair):
        pl.semaphore_signal(barrier, inc=1, device_id={"chan": chan, "pair": pair}, device_id_type=MESH)

    def greet_chip(peer):
        greet(peer * 2)
        greet(peer * 2 + 1)

    other_rows(greet_chip)
    own_row(greet_chip)
    greet(chip * 2 + 1 - core)
    for i in range(1, nchan):
        peer = lax.rem(chan + i, nchan)
        pl.semaphore_signal(barrier, inc=1, device_id={"chan": peer, "pair": me}, device_id_type=MESH)

    for load in loads:
        load.wait()

    owner = owner_ref[...]
    count = count_ref[...].astype(F32)
    slot = slot_ref[...].astype(F32)
    own_hot = jnp.where(iota((n, rows), 0) == owner, 1.0, 0.0).astype(BF16)
    before = jnp.where(iota((rows, rows), 0) < iota((rows, rows), 1), 1.0, 0.0).astype(BF16)
    rank = jnp.sum(own_hot.astype(F32) * dot(own_hot, before), axis=0, keepdims=True).astype(I32)

    lane_hit = iota((128, rows), 0) == rank
    by_slot = jnp.where(lane_hit, slot, 0.0).astype(BF16)
    by_count = jnp.where(lane_hit, count * 128.0, 0.0).astype(BF16)
    meta = dot_nt(own_hot, by_slot) + dot_nt(own_hot, by_count)
    meta_send[...] = meta.reshape(n, 1, 128)

    target_a = jnp.where(rank < 8, owner * 8 + rank, -1)
    target_b = jnp.where(rank >= 8, owner * 8 + rank - 8, -1)
    step_owners = min(16, n)
    step_rows = step_owners * 8

    def pack(i, carry):
        place = iota((step_rows, rows), 0) + i * step_rows
        pick_a = jnp.where(place == target_a, count, 0.0).astype(BF16)
        pick_b = jnp.where((place & -5) == target_b, count, 0.0).astype(BF16)
        vis = vis_ref[...]
        got_a = dot(pick_a, vis)
        got_b = dot(pick_b, vis)
        low = (iota((step_rows, 128), 0) & 4) == 0
        mixed = jnp.where(low, got_b[:, :128], got_b[:, 128:])
        at = pl.ds(i * step_owners, step_owners)
        send[at, 0] = got_a[:, :128].reshape(step_owners, 8, 128).astype(BF16)
        send[at, 1] = got_a[:, 128:].reshape(step_owners, 8, 128).astype(BF16)
        send[at, 2] = mixed.reshape(step_owners, 8, 128).astype(BF16)
        return carry

    lax.fori_loop(0, n // step_owners, pack, 0)

    pl.semaphore_wait(barrier, n - 1 + nchan - 1)

    def ship(peer):
        pltpu.make_async_remote_copy(
            send.at[peer], recv.at[me], data_s, data_r,
            device_id={"chan": chan, "pair": peer}, device_id_type=MESH).start()

    def ship_chip(peer):
        ship(peer * 2 + core)
        ship(peer * 2 + 1 - core)

    own_row(ship_chip)

    def send_meta(pair):
        pltpu.make_async_remote_copy(
            meta_send.at[pair], meta_recv.at[me], meta_s, meta_r,
            device_id={"chan": chan, "pair": pair}, device_id_type=MESH).start()

    groups = chips // nchan
    group = lax.div(chip, nchan)
    keeper = lax.rem(chip, nchan) == chan

    at_once = 5 if groups % 5 == 1 else 1

    def send_metas(i, carry):
        for j in range(at_once):
            peer = lax.rem(group + i * at_once + (j + 1), groups) * nchan + chan
            send_meta(peer * 2)
            send_meta(peer * 2 + 1)
        return carry

    lax.fori_loop(0, (groups - 1) // at_once, send_metas, 0)

    @pl.when(keeper)
    def _():
        send_meta(chip * 2 + 1 - core)
        pltpu.make_async_copy(meta_send.at[me], meta_recv.at[me], meta_r).start()

    @pl.when(jnp.logical_not(keeper))
    def _():
        send_meta((group * nchan + chan) * 2)
        send_meta((group * nchan + chan) * 2 + 1)

    other_rows(ship_chip)
    ship(chip * 2 + 1 - core)
    own_data = pltpu.make_async_copy(send.at[me], recv.at[me], data_r)
    own_data.start()

    beam_copy.wait()
    mwin, modes = beam_buf.shape[0], beam_buf.shape[3]
    base = beam_buf.shape[2]
    width = min(128, modes)
    turned = width // 2
    for m in range(mwin):
        for r in range(2):
            def turn(i, carry, m=m, r=r):
                at = pl.ds(pl.multiple_of(i * width, width), width)
                full = jnp.transpose(beam_buf[m, r, :, at])
                high = full.astype(BF16).astype(F32)
                low = full - high
                high, low = high.reshape(width // 16, 2, 8, base), low.reshape(width // 16, 2, 8, base)
                to = pl.ds(pl.multiple_of(i * turned, turned), turned)
                for half in range(2):
                    beam_t[m, half, to, r * base:(r + 1) * base] = high[:, half].reshape(turned, base).astype(BF16)
                    beam_t[m, half, to, (2 + r) * base:(3 + r) * base] = low[:, half].reshape(turned, base).astype(BF16)
                return carry

            lax.fori_loop(0, modes // width, turn, 0)

    right[:, 2 * base:, 128:] = jnp.zeros((mwin, 2 * base, 128), BF16)

    @pl.when(keeper)
    def _():
        pltpu.make_async_copy(meta_recv, meta_recv, meta_r).wait()
        for i in range(1, nchan):
            pltpu.make_async_remote_copy(
                meta_recv, meta_recv, hand_s.at[i], hand_r,
                device_id={"chan": lax.rem(chan + i, nchan), "pair": me}, device_id_type=MESH).start()

    @pl.when(jnp.logical_not(keeper))
    def _():
        pltpu.make_async_copy(meta_recv, meta_recv, hand_r).wait()

    code = jnp.transpose(meta_recv[...].reshape(n, 128))[:16]
    weight = jnp.floor(code * (1.0 / 128.0))
    place = code - weight * 128.0
    both = jnp.concatenate([place, weight], axis=0).astype(BF16)
    spread = dot(both, jnp.where(iota((n, n * 8), 0) == iota((n, n * 8), 1) // 8, 1.0, 0.0).astype(BF16))
    ranks = iota((16, n * 8), 0)
    in_message = iota((16, n * 8), 1) & 7
    at_a = ranks == in_message
    at_b = ranks == 8 + (in_message & 3)

    def flat(values, mask):
        return jnp.sum(jnp.where(mask, values, 0.0), axis=0, keepdims=True)

    slot_a, slot_b = flat(spread[:16], at_a), flat(spread[:16], at_b)
    weight_a, weight_b = flat(spread[16:], at_a), flat(spread[16:], at_b)
    first = (iota((16, n * 8), 1) & 4) == 0

    def mark(i, carry):
        at = pl.multiple_of(i * 16, 16)
        bases = (iota((16, n * 8), 0) + at).astype(F32)
        hit_a = jnp.where(bases == slot_a, 1.0, 0.0)
        hit_b = jnp.where(bases == slot_b, 1.0, 0.0)
        hit_0 = jnp.where(first, hit_b, 0.0)
        hot_a[pl.ds(at, 16)] = hit_a.astype(BF16)
        hot_b[pl.ds(at, 16)] = hit_0.astype(BF16)
        hot_b[pl.ds(base + at, 16)] = (hit_b - hit_0).astype(BF16)
        denom = jnp.sum(hit_a * weight_a + hit_0 * weight_b, axis=1, keepdims=True)
        bottom[pl.ds(at, 16)] = jnp.broadcast_to(jnp.maximum(denom, 1.0), (16, 128))
        return carry

    lax.fori_loop(0, base // 16, mark, 0)

    pltpu.make_async_copy(recv, recv, data_r).wait()

    early = jnp.concatenate([recv[:, 0].reshape(n * 8, 128), recv[:, 1].reshape(n * 8, 128)], axis=1)
    numer = dot(hot_a[...], early)
    late = dot(hot_b[...], recv[:, 2].reshape(n * 8, 128))
    numer = (numer[:, :128] + late[:base], numer[:, 128:] + late[base:])
    sign = jnp.where(iota((base, 128), 1) < sets, 1.0, -1.0)
    for m in range(mwin):
        stacked = numer[m] / bottom[...]
        swapped = jnp.concatenate([stacked[:, sets:], stacked[:, :sets]], axis=1) * sign
        for r, half in enumerate((stacked, swapped)):
            high = half.astype(BF16)
            right[m, r * base:(r + 1) * base, :128] = high
            right[m, (2 + r) * base:(3 + r) * base, :128] = high
            right[m, r * base:(r + 1) * base, 128:] = (half - high.astype(F32)).astype(BF16)

    step_modes = min(256, modes // 2)
    step_blocks = step_modes // 8

    pieces = modes // 2 // step_modes

    def project(parity, to, m, i):
        both = dot(beam_t[m, parity, i * step_modes:(i + 1) * step_modes, :], right[m])
        sums = both[:, :128] + both[:, 128:]
        part[to, m, i * step_blocks:(i + 1) * step_blocks] = sums.reshape(step_blocks, 8, 128)

    to_core = []
    for m in range(mwin):
        for i in range(pieces):
            project(1 - core, 0, m, i)
            at = pl.ds(i * step_blocks, step_blocks)
            to_core.append(pltpu.make_async_remote_copy(
                part.at[0, m, at], core_recv.at[m, at], core_s.at[m, i], core_r.at[m, i],
                device_id={"chan": chan, "pair": chip * 2 + 1 - core}, device_id_type=MESH))
            to_core[-1].start()
    for m in range(mwin):
        for i in range(pieces):
            project(core, 1, m, i)

    top = jnp.zeros((8, 128), F32)
    step_chips = min(8, step_blocks)
    for m in range(mwin):
        for i in range(pieces):
            to_core[m * pieces + i].wait_recv()

            def merge(j, top, m=m, i=i):
                at = pl.ds(i * step_blocks + j * step_chips, step_chips)
                sums = part[1, m, at] + core_recv[m, at]
                part[1, m, at] = sums
                return jnp.maximum(top, jnp.max(jnp.abs(sums), axis=0))

            top = lax.fori_loop(0, step_blocks // step_chips, merge, top)
    peak = jnp.max(jnp.max(top, axis=1, keepdims=True), axis=0, keepdims=True)
    peak = jnp.maximum(peak, 1e-30)
    scale_send[...] = jnp.broadcast_to(peak * (1.0 / 32000.0), (1, 128))
    factor = jnp.broadcast_to(32000.0 / peak, (8, 128))

    def code_sums(i, carry):
        at = pl.ds(i * step_chips, step_chips)
        scaled = jnp.concatenate([part[1, 0, at] * factor, part[1, 1, at] * factor], axis=2)
        send2[at] = jnp.round(scaled).astype(I32).astype(I16)
        return carry

    lax.fori_loop(0, chips // step_chips, code_sums, 0)

    own_scale = pltpu.make_async_copy(scale_send, scale_recv.at[chip], scale_r)
    own_scale.start()
    own_red = pltpu.make_async_copy(send2.at[chip], recv2.at[chip], red_r)
    own_red.start()

    def send_red(peer):
        target = {"chan": chan, "pair": peer * 2 + core}
        pltpu.make_async_remote_copy(
            send2.at[peer], recv2.at[chip], red_s, red_r, device_id=target, device_id_type=MESH).start()
        pltpu.make_async_remote_copy(
            scale_send, scale_recv.at[chip], scale_s, scale_r, device_id=target, device_id_type=MESH).start()

    own_row(send_red)
    first_of = [lax.rem(chip_row + far(k, depth), depth) * side for k in range(depth)]
    spots = [lax.rem(chip_spot + far(k, side), side) for k in range(side)]
    for total in range(depth + side - 2):
        for k in range(max(0, total - side + 1), min(depth - 1, total + 1)):
            send_red(first_of[k] + spots[total - k])

    pltpu.make_async_copy(scale_recv, scale_recv, scale_r).wait()
    pltpu.make_async_copy(recv2, recv2, red_r).wait()

    step_adds = min(8, chips)

    def add_up(i, sums):
        for j in range(step_adds):
            scale = scale_recv[i * step_adds + j]
            sums = sums + recv2[i * step_adds + j].astype(I32).astype(F32) * jnp.concatenate([scale, scale], axis=1)
        return sums

    total = lax.fori_loop(0, chips // step_adds, add_up, jnp.zeros((8, columns), F32))
    total_buf[...] = total
    modes_out = pltpu.make_async_copy(total_buf, result_hbm, out_sem)
    modes_out.start()
    square = total * total
    power_0 = jnp.sum(square[:, :128], axis=1, keepdims=True)
    power_1 = jnp.sum(square[:, 128:], axis=1, keepdims=True)
    pow_send[...] = jnp.where(iota((8, 128), 1) == 0, power_0, power_1)
    own_power = pltpu.make_async_copy(pow_send, power_hbm.at[chan], own_sem)
    own_power.start()
    sends = []
    for i in range(1, nchan):
        peer = lax.rem(chan + i, nchan)
        copy = pltpu.make_async_remote_copy(
            pow_send, power_hbm.at[chan], pow_s.at[i], pow_r.at[i],
            device_id={"chan": peer, "pair": me}, device_id_type=MESH)
        copy.start()
        sends.append(copy)
    for copy in sends:
        copy.wait()
    own_power.wait()
    modes_out.wait()

    for copy in to_core:
        copy.wait_send()
    sent = 2 * groups

    @pl.when(keeper)
    def _():
        pltpu.make_async_copy(meta_send.at[pl.ds(0, sent - 1)], meta_send.at[pl.ds(0, sent - 1)], meta_s).wait()
        for i in range(1, nchan):
            pltpu.make_async_copy(meta_recv, meta_recv, hand_s.at[i]).wait()

    @pl.when(jnp.logical_not(keeper))
    def _():
        pltpu.make_async_copy(meta_send.at[pl.ds(0, sent)], meta_send.at[pl.ds(0, sent)], meta_s).wait()

    pltpu.make_async_copy(send.at[pl.ds(1, n - 1)], send.at[pl.ds(1, n - 1)], data_s).wait()
    pltpu.make_async_copy(send2.at[pl.ds(1, chips - 1)], send2.at[pl.ds(1, chips - 1)], red_s).wait()
    pltpu.make_async_copy(scale_recv.at[pl.ds(1, chips - 1)], scale_recv.at[pl.ds(1, chips - 1)], scale_s).wait()


def shape_results(mwin, sets, result_ref, powers_ref, modes_ref, power_ref):
    for m in range(mwin):
        for part in range(2):
            at = (2 * m + part) * sets
            modes_ref[:, m, part, :] = result_ref[:, at:at + sets]
    power = jnp.sum(powers_ref[...], axis=0) * (1.0 / (powers_ref.shape[0] * sets))
    power_ref[...] = jnp.transpose(power)[:mwin]


def per_device(visibility, pair_counts, owner_ids, slot_ids, beam):
    n, nchan = lax.axis_size("pair"), lax.axis_size("chan")
    rows, columns = visibility.shape[1:]
    mwin, _, base, modes = beam.shape[1:]
    sets = columns // (2 * mwin)
    chips = n // 2
    vmem, hbm = pl.BlockSpec(memory_space=pltpu.VMEM), pl.BlockSpec(memory_space=pltpu.HBM)
    dma = pltpu.SemaphoreType.DMA
    amplitudes, powers = pl.pallas_call(
        functools.partial(body, n, nchan, sets),
        out_shape=(
            jax.ShapeDtypeStruct((8, columns), F32),
            jax.ShapeDtypeStruct((nchan, 8, 128), F32),
        ),
        in_specs=[hbm] * 5,
        out_specs=(hbm, hbm),
        scratch_shapes=[
            pltpu.VMEM((1, rows), I32),
            pltpu.VMEM((1, rows), I32),
            pltpu.VMEM((1, rows), I32),
            pltpu.VMEM((rows, columns), BF16),
            pltpu.VMEM((n, 3, 8, 128), BF16),
            pltpu.VMEM((n, 3, 8, 128), BF16),
            pltpu.VMEM((n, 1, 128), F32),
            pltpu.VMEM((n, 1, 128), F32),
            pltpu.VMEM((mwin, 2, base, modes), F32),
            pltpu.VMEM((mwin, 2, modes // 2, 4 * base), BF16),
            pltpu.VMEM((base, n * 8), BF16),
            pltpu.VMEM((2 * base, n * 8), BF16),
            pltpu.VMEM((base, 128), F32),
            pltpu.VMEM((mwin, 4 * base, 256), BF16),
            pltpu.VMEM((2, mwin, chips, 8, 128), F32),
            pltpu.VMEM((mwin, chips, 8, 128), F32),
            pltpu.VMEM((chips, 8, columns), I16),
            pltpu.VMEM((chips, 8, columns), I16),
            pltpu.VMEM((1, 128), F32),
            pltpu.VMEM((chips, 1, 128), F32),
            pltpu.VMEM((8, columns), F32),
            pltpu.VMEM((8, 128), F32),
            dma((4,)), dma, dma, dma, dma((nchan,)), dma, dma, dma, dma((mwin, 2)), dma((mwin, 2)), dma, dma, dma, dma,
            dma((nchan,)), dma((nchan,)), dma, dma,
        ],
        compiler_params=pltpu.CompilerParams(
            collective_id=0, has_side_effects=True
        ),
        name="stack_project",
    )(
        owner_ids.reshape(1, rows), slot_ids.reshape(1, rows), pair_counts.reshape(1, rows),
        visibility[0], beam[0],
    )
    shaped, power = pl.pallas_call(
        functools.partial(shape_results, mwin, sets),
        out_shape=(jax.ShapeDtypeStruct((8, mwin, 2, sets), F32), jax.ShapeDtypeStruct((mwin, 8), F32)),
        in_specs=[vmem] * 2,
        out_specs=(vmem, vmem),
        name="shape_results",
    )(amplitudes, powers)
    return shaped[None], power.T


def solution(mesh):
    in_specs = (
        P("chan", "pair", None),
        P("pair"),
        P("pair", None),
        P("pair"),
        P("chan", None, None, "pair", None),
    )
    out_specs = (P("chan", "pair", None, None, None), P("pair", None))
    return jax.shard_map(
        per_device, mesh=mesh, in_specs=in_specs, out_specs=out_specs, check_vma=False
    )
```

```python
import functools

import jax
import jax.numpy as jnp
from jax import lax
from jax.experimental import pallas as pl
from jax.experimental.pallas import tpu as pltpu
from jax.sharding import PartitionSpec as P

MESH = pl.DeviceIdType.MESH
F32, BF16, I32, I16 = jnp.float32, jnp.bfloat16, jnp.int32, jnp.int16


def iota(shape, axis):
    return lax.broadcasted_iota(I32, shape, axis)


def dot(a, b):
    return jnp.dot(a, b, preferred_element_type=F32)


def dot_nt(a, b):
    return lax.dot_general(a, b, (((1,), (1,)), ((), ())), preferred_element_type=F32)


def body(
    n, nchan, sets,
    owner_hbm, slot_hbm, count_hbm, vis_hbm, beam_hbm,
    result_hbm, power_hbm,
    owner_ref, slot_ref, count_ref, vis_ref,
    send, recv, meta_send, meta_recv,
    beam_buf, beam_t, hot_a, hot_b, bottom, right,
    part, core_recv, send2, recv2, scale_send, scale_recv, total_buf, pow_send,
    in_sem, beam_sem, meta_s, meta_r, hand_s, hand_r, data_s, data_r, core_s, core_r, red_s, red_r, scale_s, scale_r, pow_s, pow_r, out_sem, own_sem,
):
    chan = lax.axis_index("chan")
    me = lax.axis_index("pair")
    chips = n // 2
    chip, core = me // 2, me % 2
    rows, columns = vis_ref.shape
    step_chips = min(8, chips)

    loads = [
        pltpu.make_async_copy(src, dst, in_sem.at[i])
        for i, (src, dst) in enumerate((
            (owner_hbm, owner_ref), (slot_hbm, slot_ref), (count_hbm, count_ref), (vis_hbm, vis_ref),
        ))
    ]
    for load in loads:
        load.start()
    beam_copy = pltpu.make_async_copy(beam_hbm, beam_buf, beam_sem)
    beam_copy.start()

    barrier = pltpu.get_barrier_semaphore()

    side = 8
    while side * side > chips:
        side //= 2
    depth = chips // side
    chip_row, chip_spot = lax.div(chip, side), lax.rem(chip, side)

    turn_sign = 1 - 2 * core

    def far(k, size):
        half = lax.div(k, 2) if not isinstance(k, int) else k // 2
        return size // 2 + turn_sign * (half - (k - 2 * half) * (2 * half + 1))

    def own_row(visit):
        for k in range(side - 1):
            visit(chip_row * side + lax.rem(chip_spot + far(k, side), side))

    def other_rows(visit):
        def diagonal(total, carry):
            def step(k, carry):
                line = lax.rem(chip_row + far(k, depth), depth)
                visit(line * side + lax.rem(chip_spot + far(total - k, side), side))
                return carry

            return lax.fori_loop(lax.max(0, total - side + 1), lax.min(depth - 1, total + 1), step, carry)

        lax.fori_loop(0, depth + side - 2, diagonal, 0)

    def greet(pair):
        pl.semaphore_signal(barrier, inc=1, device_id={"chan": chan, "pair": pair}, device_id_type=MESH)

    def greet_chip(peer):
        greet(peer * 2)
        greet(peer * 2 + 1)

    other_rows(greet_chip)
    own_row(greet_chip)
    greet(chip * 2 + 1 - core)
    for i in range(1, nchan):
        peer = lax.rem(chan + i, nchan)
        pl.semaphore_signal(barrier, inc=1, device_id={"chan": peer, "pair": me}, device_id_type=MESH)

    for load in loads:
        load.wait()

    owner = owner_ref[...]
    count = count_ref[...].astype(F32)
    slot = slot_ref[...].astype(F32)
    own_hot = jnp.where(iota((n, rows), 0) == owner, 1.0, 0.0).astype(BF16)
    before = jnp.where(iota((rows, rows), 0) < iota((rows, rows), 1), 1.0, 0.0).astype(BF16)
    rank = jnp.sum(own_hot.astype(F32) * dot(own_hot, before), axis=0, keepdims=True).astype(I32)

    lane_hit = iota((128, rows), 0) == rank
    by_slot = jnp.where(lane_hit, slot, 0.0).astype(BF16)
    by_count = jnp.where(lane_hit, count * 128.0, 0.0).astype(BF16)
    meta = dot_nt(own_hot, by_slot) + dot_nt(own_hot, by_count)
    meta_send[...] = meta.reshape(n, 1, 128)

    target_a = jnp.where(rank < 8, owner * 8 + rank, -1)
    target_b = jnp.where(rank >= 8, owner * 8 + rank - 8, -1)
    step_owners = min(16, n)
    step_rows = step_owners * 8

    def pack(i, carry):
        place = iota((step_rows, rows), 0) + i * step_rows
        pick_a = jnp.where(place == target_a, count, 0.0).astype(BF16)
        pick_b = jnp.where((place & -5) == target_b, count, 0.0).astype(BF16)
        vis = vis_ref[...]
        got_a = dot(pick_a, vis)
        got_b = dot(pick_b, vis)
        low = (iota((step_rows, 128), 0) & 4) == 0
        mixed = jnp.where(low, got_b[:, :128], got_b[:, 128:])
        at = pl.ds(i * step_owners, step_owners)
        send[at, 0] = got_a[:, :128].reshape(step_owners, 8, 128).astype(BF16)
        send[at, 1] = got_a[:, 128:].reshape(step_owners, 8, 128).astype(BF16)
        send[at, 2] = mixed.reshape(step_owners, 8, 128).astype(BF16)
        return carry

    lax.fori_loop(0, n // step_owners, pack, 0)

    pl.semaphore_wait(barrier, n - 1 + nchan - 1)

    def ship(peer):
        pltpu.make_async_remote_copy(
            send.at[peer], recv.at[me], data_s, data_r,
            device_id={"chan": chan, "pair": peer}, device_id_type=MESH).start()

    def ship_chip(peer):
        ship(peer * 2 + core)
        ship(peer * 2 + 1 - core)

    own_row(ship_chip)

    def send_meta(pair):
        pltpu.make_async_remote_copy(
            meta_send.at[pair], meta_recv.at[me], meta_s, meta_r,
            device_id={"chan": chan, "pair": pair}, device_id_type=MESH).start()

    groups = chips // nchan
    group = lax.div(chip, nchan)
    keeper = lax.rem(chip, nchan) == chan

    at_once = 5 if groups % 5 == 1 else 1

    def send_metas(i, carry):
        for j in range(at_once):
            peer = lax.rem(group + i * at_once + (j + 1), groups) * nchan + chan
            send_meta(peer * 2)
            send_meta(peer * 2 + 1)
        return carry

    lax.fori_loop(0, (groups - 1) // at_once, send_metas, 0)

    @pl.when(keeper)
    def _():
        send_meta(chip * 2 + 1 - core)
        pltpu.make_async_copy(meta_send.at[me], meta_recv.at[me], meta_r).start()

    @pl.when(jnp.logical_not(keeper))
    def _():
        send_meta((group * nchan + chan) * 2)
        send_meta((group * nchan + chan) * 2 + 1)

    other_rows(ship_chip)
    ship(chip * 2 + 1 - core)
    own_data = pltpu.make_async_copy(send.at[me], recv.at[me], data_r)
    own_data.start()

    beam_copy.wait()
    mwin, modes = beam_buf.shape[0], beam_buf.shape[3]
    base = beam_buf.shape[2]
    width = min(128, modes)
    turned = width // 2
    for m in range(mwin):
        for r in range(2):
            def turn(i, carry, m=m, r=r):
                at = pl.ds(pl.multiple_of(i * width, width), width)
                full = jnp.transpose(beam_buf[m, r, :, at])
                high = full.astype(BF16).astype(F32)
                low = full - high
                high, low = high.reshape(width // 16, 2, 8, base), low.reshape(width // 16, 2, 8, base)
                to = pl.ds(pl.multiple_of(i * turned, turned), turned)
                for half in range(2):
                    beam_t[m, half, to, r * base:(r + 1) * base] = high[:, half].reshape(turned, base).astype(BF16)
                    beam_t[m, half, to, (2 + r) * base:(3 + r) * base] = low[:, half].reshape(turned, base).astype(BF16)
                return carry

            lax.fori_loop(0, modes // width, turn, 0)

    right[:, 2 * base:, 128:] = jnp.zeros((mwin, 2 * base, 128), BF16)

    @pl.when(keeper)
    def _():
        pltpu.make_async_copy(meta_recv, meta_recv, meta_r).wait()
        for i in range(1, nchan):
            pltpu.make_async_remote_copy(
                meta_recv, meta_recv, hand_s.at[i], hand_r,
                device_id={"chan": lax.rem(chan + i, nchan), "pair": me}, device_id_type=MESH).start()

    @pl.when(jnp.logical_not(keeper))
    def _():
        pltpu.make_async_copy(meta_recv, meta_recv, hand_r).wait()

    code = jnp.transpose(meta_recv[...].reshape(n, 128))[:16]
    weight = jnp.floor(code * (1.0 / 128.0))
    place = code - weight * 128.0
    both = jnp.concatenate([place, weight], axis=0).astype(BF16)
    spread = dot(both, jnp.where(iota((n, n * 8), 0) == iota((n, n * 8), 1) // 8, 1.0, 0.0).astype(BF16))
    ranks = iota((16, n * 8), 0)
    in_message = iota((16, n * 8), 1) & 7
    at_a = ranks == in_message
    at_b = ranks == 8 + (in_message & 3)

    def flat(values, mask):
        return jnp.sum(jnp.where(mask, values, 0.0), axis=0, keepdims=True)

    slot_a, slot_b = flat(spread[:16], at_a), flat(spread[:16], at_b)
    weight_a, weight_b = flat(spread[16:], at_a), flat(spread[16:], at_b)
    first = (iota((16, n * 8), 1) & 4) == 0

    def mark(i, carry):
        at = pl.multiple_of(i * 16, 16)
        bases = (iota((16, n * 8), 0) + at).astype(F32)
        hit_a = jnp.where(bases == slot_a, 1.0, 0.0)
        hit_b = jnp.where(bases == slot_b, 1.0, 0.0)
        hit_0 = jnp.where(first, hit_b, 0.0)
        hot_a[pl.ds(at, 16)] = hit_a.astype(BF16)
        hot_b[pl.ds(at, 16)] = hit_0.astype(BF16)
        hot_b[pl.ds(base + at, 16)] = (hit_b - hit_0).astype(BF16)
        denom = jnp.sum(hit_a * weight_a + hit_0 * weight_b, axis=1, keepdims=True)
        bottom[pl.ds(at, 16)] = jnp.broadcast_to(jnp.maximum(denom, 1.0), (16, 128))
        return carry

    lax.fori_loop(0, base // 16, mark, 0)

    pltpu.make_async_copy(recv, recv, data_r).wait()

    early = jnp.concatenate([recv[:, 0].reshape(n * 8, 128), recv[:, 1].reshape(n * 8, 128)], axis=1)
    numer = dot(hot_a[...], early)
    late = dot(hot_b[...], recv[:, 2].reshape(n * 8, 128))
    numer = (numer[:, :128] + late[:base], numer[:, 128:] + late[base:])
    sign = jnp.where(iota((base, 128), 1) < sets, 1.0, -1.0)
    for m in range(mwin):
        stacked = numer[m] / bottom[...]
        swapped = jnp.concatenate([stacked[:, sets:], stacked[:, :sets]], axis=1) * sign
        for r, half in enumerate((stacked, swapped)):
            high = half.astype(BF16)
            right[m, r * base:(r + 1) * base, :128] = high
            right[m, (2 + r) * base:(3 + r) * base, :128] = high
            right[m, r * base:(r + 1) * base, 128:] = (half - high.astype(F32)).astype(BF16)

    step_modes = min(256, modes // 2)
    step_blocks = step_modes // 8

    pieces = modes // 2 // step_modes

    def project(parity, to, m, i):
        both = dot(beam_t[m, parity, i * step_modes:(i + 1) * step_modes, :], right[m])
        sums = both[:, :128] + both[:, 128:]
        part[to, m, i * step_blocks:(i + 1) * step_blocks] = sums.reshape(step_blocks, 8, 128)

    to_core = []
    for m in range(mwin):
        for i in range(pieces):
            project(1 - core, 0, m, i)
            at = pl.ds(i * step_blocks, step_blocks)
            to_core.append(pltpu.make_async_remote_copy(
                part.at[0, m, at], core_recv.at[m, at], core_s.at[m, i], core_r.at[m, i],
                device_id={"chan": chan, "pair": chip * 2 + 1 - core}, device_id_type=MESH))
            to_core[-1].start()
    for m in range(mwin):
        for i in range(pieces):
            project(core, 1, m, i)

    top = jnp.zeros((8, 128), F32)
    step_chips = min(8, step_blocks)
    for m in range(mwin):
        for i in range(pieces):
            to_core[m * pieces + i].wait_recv()

            def merge(j, top, m=m, i=i):
                at = pl.ds(i * step_blocks + j * step_chips, step_chips)
                sums = part[1, m, at] + core_recv[m, at]
                part[1, m, at] = sums
                return jnp.maximum(top, jnp.max(jnp.abs(sums), axis=0))

            top = lax.fori_loop(0, step_blocks // step_chips, merge, top)
    peak = jnp.max(jnp.max(top, axis=1, keepdims=True), axis=0, keepdims=True)
    peak = jnp.maximum(peak, 1e-30)
    scale_send[...] = jnp.broadcast_to(peak * (1.0 / 32000.0), (1, 128))
    factor = jnp.broadcast_to(32000.0 / peak, (8, 128))

    def code_sums(i, carry):
        at = pl.ds(i * step_chips, step_chips)
        scaled = jnp.concatenate([part[1, 0, at] * factor, part[1, 1, at] * factor], axis=2)
        send2[at] = jnp.round(scaled).astype(I32).astype(I16)
        return carry

    lax.fori_loop(0, chips // step_chips, code_sums, 0)

    own_scale = pltpu.make_async_copy(scale_send, scale_recv.at[chip], scale_r)
    own_scale.start()
    own_red = pltpu.make_async_copy(send2.at[chip], recv2.at[chip], red_r)
    own_red.start()

    def send_red(peer):
        target = {"chan": chan, "pair": peer * 2 + core}
        pltpu.make_async_remote_copy(
            send2.at[peer], recv2.at[chip], red_s, red_r, device_id=target, device_id_type=MESH).start()
        pltpu.make_async_remote_copy(
            scale_send, scale_recv.at[chip], scale_s, scale_r, device_id=target, device_id_type=MESH).start()

    own_row(send_red)
    other_rows(send_red)

    pltpu.make_async_copy(scale_recv, scale_recv, scale_r).wait()
    pltpu.make_async_copy(recv2, recv2, red_r).wait()

    step_adds = min(8, chips)

    def add_up(i, sums):
        for j in range(step_adds):
            scale = scale_recv[i * step_adds + j]
            sums = sums + recv2[i * step_adds + j].astype(I32).astype(F32) * jnp.concatenate([scale, scale], axis=1)
        return sums

    total = lax.fori_loop(0, chips // step_adds, add_up, jnp.zeros((8, columns), F32))
    total_buf[...] = total
    modes_out = pltpu.make_async_copy(total_buf, result_hbm, out_sem)
    modes_out.start()
    square = total * total
    power_0 = jnp.sum(square[:, :128], axis=1, keepdims=True)
    power_1 = jnp.sum(square[:, 128:], axis=1, keepdims=True)
    pow_send[...] = jnp.where(iota((8, 128), 1) == 0, power_0, power_1)
    own_power = pltpu.make_async_copy(pow_send, power_hbm.at[chan], own_sem)
    own_power.start()
    sends = []
    for i in range(1, nchan):
        peer = lax.rem(chan + i, nchan)
        copy = pltpu.make_async_remote_copy(
            pow_send, power_hbm.at[chan], pow_s.at[i], pow_r.at[i],
            device_id={"chan": peer, "pair": me}, device_id_type=MESH)
        copy.start()
        sends.append(copy)
    for copy in sends:
        copy.wait()
    own_power.wait()
    modes_out.wait()

    for copy in to_core:
        copy.wait_send()
    sent = 2 * groups

    @pl.when(keeper)
    def _():
        pltpu.make_async_copy(meta_send.at[pl.ds(0, sent - 1)], meta_send.at[pl.ds(0, sent - 1)], meta_s).wait()
        for i in range(1, nchan):
            pltpu.make_async_copy(meta_recv, meta_recv, hand_s.at[i]).wait()

    @pl.when(jnp.logical_not(keeper))
    def _():
        pltpu.make_async_copy(meta_send.at[pl.ds(0, sent)], meta_send.at[pl.ds(0, sent)], meta_s).wait()

    pltpu.make_async_copy(send.at[pl.ds(1, n - 1)], send.at[pl.ds(1, n - 1)], data_s).wait()
    pltpu.make_async_copy(send2.at[pl.ds(1, chips - 1)], send2.at[pl.ds(1, chips - 1)], red_s).wait()
    pltpu.make_async_copy(scale_recv.at[pl.ds(1, chips - 1)], scale_recv.at[pl.ds(1, chips - 1)], scale_s).wait()


def shape_results(mwin, sets, result_ref, powers_ref, modes_ref, power_ref):
    for m in range(mwin):
        for part in range(2):
            at = (2 * m + part) * sets
            modes_ref[:, m, part, :] = result_ref[:, at:at + sets]
    power = jnp.sum(powers_ref[...], axis=0) * (1.0 / (powers_ref.shape[0] * sets))
    power_ref[...] = jnp.transpose(power)[:mwin]


def per_device(visibility, pair_counts, owner_ids, slot_ids, beam):
    n, nchan = lax.axis_size("pair"), lax.axis_size("chan")
    rows, columns = visibility.shape[1:]
    mwin, _, base, modes = beam.shape[1:]
    sets = columns // (2 * mwin)
    chips = n // 2
    vmem, hbm = pl.BlockSpec(memory_space=pltpu.VMEM), pl.BlockSpec(memory_space=pltpu.HBM)
    dma = pltpu.SemaphoreType.DMA
    amplitudes, powers = pl.pallas_call(
        functools.partial(body, n, nchan, sets),
        out_shape=(
            jax.ShapeDtypeStruct((8, columns), F32),
            jax.ShapeDtypeStruct((nchan, 8, 128), F32),
        ),
        in_specs=[hbm] * 5,
        out_specs=(hbm, hbm),
        scratch_shapes=[
            pltpu.VMEM((1, rows), I32),
            pltpu.VMEM((1, rows), I32),
            pltpu.VMEM((1, rows), I32),
            pltpu.VMEM((rows, columns), BF16),
            pltpu.VMEM((n, 3, 8, 128), BF16),
            pltpu.VMEM((n, 3, 8, 128), BF16),
            pltpu.VMEM((n, 1, 128), F32),
            pltpu.VMEM((n, 1, 128), F32),
            pltpu.VMEM((mwin, 2, base, modes), F32),
            pltpu.VMEM((mwin, 2, modes // 2, 4 * base), BF16),
            pltpu.VMEM((base, n * 8), BF16),
            pltpu.VMEM((2 * base, n * 8), BF16),
            pltpu.VMEM((base, 128), F32),
            pltpu.VMEM((mwin, 4 * base, 256), BF16),
            pltpu.VMEM((2, mwin, chips, 8, 128), F32),
            pltpu.VMEM((mwin, chips, 8, 128), F32),
            pltpu.VMEM((chips, 8, columns), I16),
            pltpu.VMEM((chips, 8, columns), I16),
            pltpu.VMEM((1, 128), F32),
            pltpu.VMEM((chips, 1, 128), F32),
            pltpu.VMEM((8, columns), F32),
            pltpu.VMEM((8, 128), F32),
            dma((4,)), dma, dma, dma, dma((nchan,)), dma, dma, dma, dma((mwin, 2)), dma((mwin, 2)), dma, dma, dma, dma,
            dma((nchan,)), dma((nchan,)), dma, dma,
        ],
        compiler_params=pltpu.CompilerParams(
            collective_id=0, has_side_effects=True
        ),
        name="stack_project",
    )(
        owner_ids.reshape(1, rows), slot_ids.reshape(1, rows), pair_counts.reshape(1, rows),
        visibility[0], beam[0],
    )
    shaped, power = pl.pallas_call(
        functools.partial(shape_results, mwin, sets),
        out_shape=(jax.ShapeDtypeStruct((8, mwin, 2, sets), F32), jax.ShapeDtypeStruct((mwin, 8), F32)),
        in_specs=[vmem] * 2,
        out_specs=(vmem, vmem),
        name="shape_results",
    )(amplitudes, powers)
    return shaped[None], power.T


def solution(mesh):
    in_specs = (
        P("chan", "pair", None),
        P("pair"),
        P("pair", None),
        P("pair"),
        P("chan", None, None, "pair", None),
    )
    out_specs = (P("chan", "pair", None, None, None), P("pair", None))
    return jax.shard_map(
        per_device, mesh=mesh, in_specs=in_specs, out_specs=out_specs, check_vma=False
    )
```

```python
import functools

import jax
import jax.numpy as jnp
from jax import lax
from jax.experimental import pallas as pl
from jax.experimental.pallas import tpu as pltpu
from jax.sharding import PartitionSpec as P

MESH = pl.DeviceIdType.MESH
F32, BF16, I32, I16 = jnp.float32, jnp.bfloat16, jnp.int32, jnp.int16


def iota(shape, axis):
    return lax.broadcasted_iota(I32, shape, axis)


def dot(a, b):
    return jnp.dot(a, b, preferred_element_type=F32)


def dot_nt(a, b):
    return lax.dot_general(a, b, (((1,), (1,)), ((), ())), preferred_element_type=F32)


def body(
    n, nchan, sets,
    owner_hbm, slot_hbm, count_hbm, vis_hbm, beam_hbm,
    result_hbm, power_hbm,
    owner_ref, slot_ref, count_ref, vis_ref,
    send, recv, meta_send, meta_recv,
    beam_buf, beam_t, hot_a, hot_b, bottom, right,
    part, core_recv, send2, recv2, scale_send, scale_recv, total_buf, pow_send,
    in_sem, beam_sem, meta_s, meta_r, hand_s, hand_r, data_s, data_r, core_s, core_r, red_s, red_r, scale_s, scale_r, pow_s, pow_r, out_sem, own_sem,
):
    chan = lax.axis_index("chan")
    me = lax.axis_index("pair")
    chips = n // 2
    chip, core = me // 2, me % 2
    rows, columns = vis_ref.shape
    step_chips = min(8, chips)

    loads = [
        pltpu.make_async_copy(src, dst, in_sem.at[i])
        for i, (src, dst) in enumerate((
            (owner_hbm, owner_ref), (slot_hbm, slot_ref), (count_hbm, count_ref), (vis_hbm, vis_ref),
        ))
    ]
    for load in loads:
        load.start()
    beam_copy = pltpu.make_async_copy(beam_hbm, beam_buf, beam_sem)
    beam_copy.start()

    barrier = pltpu.get_barrier_semaphore()

    side = 8
    while side * side > chips:
        side //= 2
    depth = chips // side
    chip_row, chip_spot = lax.div(chip, side), lax.rem(chip, side)

    turn_sign = 1 - 2 * core

    def far(k, size):
        half = lax.div(k, 2) if not isinstance(k, int) else k // 2
        return size // 2 + turn_sign * (half - (k - 2 * half) * (2 * half + 1))

    def own_row(visit):
        for k in range(side - 1):
            visit(chip_row * side + lax.rem(chip_spot + far(k, side), side))

    def other_rows(visit):
        def diagonal(total, carry):
            def step(k, carry):
                line = lax.rem(chip_row + far(k, depth), depth)
                visit(line * side + lax.rem(chip_spot + far(total - k, side), side))
                return carry

            return lax.fori_loop(lax.max(0, total - side + 1), lax.min(depth - 1, total + 1), step, carry)

        lax.fori_loop(0, depth + side - 2, diagonal, 0)

    def each_chip(visit):
        own_row(visit)
        other_rows(visit)

    def greet(pair):
        pl.semaphore_signal(barrier, inc=1, device_id={"chan": chan, "pair": pair}, device_id_type=MESH)

    def greet_chip(peer):
        greet(peer * 2)
        greet(peer * 2 + 1)

    other_rows(greet_chip)
    own_row(greet_chip)
    greet(chip * 2 + 1 - core)
    for i in range(1, nchan):
        peer = lax.rem(chan + i, nchan)
        pl.semaphore_signal(barrier, inc=1, device_id={"chan": peer, "pair": me}, device_id_type=MESH)

    for load in loads:
        load.wait()

    owner = owner_ref[...]
    count = count_ref[...].astype(F32)
    slot = slot_ref[...].astype(F32)
    own_hot = jnp.where(iota((n, rows), 0) == owner, 1.0, 0.0).astype(BF16)
    before = jnp.where(iota((rows, rows), 0) < iota((rows, rows), 1), 1.0, 0.0).astype(BF16)
    rank = jnp.sum(own_hot.astype(F32) * dot(own_hot, before), axis=0, keepdims=True).astype(I32)

    lane_hit = iota((128, rows), 0) == rank
    by_slot = jnp.where(lane_hit, slot, 0.0).astype(BF16)
    by_count = jnp.where(lane_hit, count * 128.0, 0.0).astype(BF16)
    meta = dot_nt(own_hot, by_slot) + dot_nt(own_hot, by_count)
    meta_send[...] = meta.reshape(n, 1, 128)

    target_a = jnp.where(rank < 8, owner * 8 + rank, -1)
    target_b = jnp.where(rank >= 8, owner * 8 + rank - 8, -1)
    step_owners = min(16, n)
    step_rows = step_owners * 8

    def pack(i, carry):
        place = iota((step_rows, rows), 0) + i * step_rows
        pick_a = jnp.where(place == target_a, count, 0.0).astype(BF16)
        pick_b = jnp.where((place & -5) == target_b, count, 0.0).astype(BF16)
        vis = vis_ref[...]
        got_a = dot(pick_a, vis)
        got_b = dot(pick_b, vis)
        low = (iota((step_rows, 128), 0) & 4) == 0
        mixed = jnp.where(low, got_b[:, :128], got_b[:, 128:])
        at = pl.ds(i * step_owners, step_owners)
        send[at, 0] = got_a[:, :128].reshape(step_owners, 8, 128).astype(BF16)
        send[at, 1] = got_a[:, 128:].reshape(step_owners, 8, 128).astype(BF16)
        send[at, 2] = mixed.reshape(step_owners, 8, 128).astype(BF16)
        return carry

    lax.fori_loop(0, n // step_owners, pack, 0)

    pl.semaphore_wait(barrier, n - 1 + nchan - 1)

    def send_meta(pair):
        pltpu.make_async_remote_copy(
            meta_send.at[pair], meta_recv.at[me], meta_s, meta_r,
            device_id={"chan": chan, "pair": pair}, device_id_type=MESH).start()

    groups = chips // nchan
    group = lax.div(chip, nchan)
    keeper = lax.rem(chip, nchan) == chan

    at_once = 5 if groups % 5 == 1 else 1

    def send_metas(i, carry):
        for j in range(at_once):
            peer = lax.rem(group + i * at_once + (j + 1), groups) * nchan + chan
            send_meta(peer * 2)
            send_meta(peer * 2 + 1)
        return carry

    lax.fori_loop(0, (groups - 1) // at_once, send_metas, 0)

    @pl.when(keeper)
    def _():
        send_meta(chip * 2 + 1 - core)
        pltpu.make_async_copy(meta_send.at[me], meta_recv.at[me], meta_r).start()

    @pl.when(jnp.logical_not(keeper))
    def _():
        send_meta((group * nchan + chan) * 2)
        send_meta((group * nchan + chan) * 2 + 1)

    own_data = pltpu.make_async_copy(send.at[me], recv.at[me], data_r)
    own_data.start()

    def ship(peer):
        pltpu.make_async_remote_copy(
            send.at[peer], recv.at[me], data_s, data_r,
            device_id={"chan": chan, "pair": peer}, device_id_type=MESH).start()

    def ship_chip(peer):
        ship(peer * 2 + core)
        ship(peer * 2 + 1 - core)

    each_chip(ship_chip)
    ship(chip * 2 + 1 - core)

    beam_copy.wait()
    mwin, modes = beam_buf.shape[0], beam_buf.shape[3]
    base = beam_buf.shape[2]
    width = min(128, modes)
    turned = width // 2
    for m in range(mwin):
        for r in range(2):
            def turn(i, carry, m=m, r=r):
                at = pl.ds(pl.multiple_of(i * width, width), width)
                full = jnp.transpose(beam_buf[m, r, :, at])
                high = full.astype(BF16).astype(F32)
                low = full - high
                high, low = high.reshape(width // 16, 2, 8, base), low.reshape(width // 16, 2, 8, base)
                to = pl.ds(pl.multiple_of(i * turned, turned), turned)
                for half in range(2):
                    beam_t[m, half, to, r * base:(r + 1) * base] = high[:, half].reshape(turned, base).astype(BF16)
                    beam_t[m, half, to, (2 + r) * base:(3 + r) * base] = low[:, half].reshape(turned, base).astype(BF16)
                return carry

            lax.fori_loop(0, modes // width, turn, 0)

    right[:, 2 * base:, 128:] = jnp.zeros((mwin, 2 * base, 128), BF16)

    @pl.when(keeper)
    def _():
        pltpu.make_async_copy(meta_recv, meta_recv, meta_r).wait()
        for i in range(1, nchan):
            pltpu.make_async_remote_copy(
                meta_recv, meta_recv, hand_s.at[i], hand_r,
                device_id={"chan": lax.rem(chan + i, nchan), "pair": me}, device_id_type=MESH).start()

    @pl.when(jnp.logical_not(keeper))
    def _():
        pltpu.make_async_copy(meta_recv, meta_recv, hand_r).wait()

    code = jnp.transpose(meta_recv[...].reshape(n, 128))[:16]
    weight = jnp.floor(code * (1.0 / 128.0))
    place = code - weight * 128.0
    both = jnp.concatenate([place, weight], axis=0).astype(BF16)
    spread = dot(both, jnp.where(iota((n, n * 8), 0) == iota((n, n * 8), 1) // 8, 1.0, 0.0).astype(BF16))
    ranks = iota((16, n * 8), 0)
    in_message = iota((16, n * 8), 1) & 7
    at_a = ranks == in_message
    at_b = ranks == 8 + (in_message & 3)

    def flat(values, mask):
        return jnp.sum(jnp.where(mask, values, 0.0), axis=0, keepdims=True)

    slot_a, slot_b = flat(spread[:16], at_a), flat(spread[:16], at_b)
    weight_a, weight_b = flat(spread[16:], at_a), flat(spread[16:], at_b)
    first = (iota((16, n * 8), 1) & 4) == 0

    def mark(i, carry):
        at = pl.multiple_of(i * 16, 16)
        bases = (iota((16, n * 8), 0) + at).astype(F32)
        hit_a = jnp.where(bases == slot_a, 1.0, 0.0)
        hit_b = jnp.where(bases == slot_b, 1.0, 0.0)
        hit_0 = jnp.where(first, hit_b, 0.0)
        hot_a[pl.ds(at, 16)] = hit_a.astype(BF16)
        hot_b[pl.ds(at, 16)] = hit_0.astype(BF16)
        hot_b[pl.ds(base + at, 16)] = (hit_b - hit_0).astype(BF16)
        denom = jnp.sum(hit_a * weight_a + hit_0 * weight_b, axis=1, keepdims=True)
        bottom[pl.ds(at, 16)] = jnp.broadcast_to(jnp.maximum(denom, 1.0), (16, 128))
        return carry

    lax.fori_loop(0, base // 16, mark, 0)

    pltpu.make_async_copy(recv, recv, data_r).wait()

    early = jnp.concatenate([recv[:, 0].reshape(n * 8, 128), recv[:, 1].reshape(n * 8, 128)], axis=1)
    numer = dot(hot_a[...], early)
    late = dot(hot_b[...], recv[:, 2].reshape(n * 8, 128))
    numer = (numer[:, :128] + late[:base], numer[:, 128:] + late[base:])
    sign = jnp.where(iota((base, 128), 1) < sets, 1.0, -1.0)
    for m in range(mwin):
        stacked = numer[m] / bottom[...]
        swapped = jnp.concatenate([stacked[:, sets:], stacked[:, :sets]], axis=1) * sign
        for r, half in enumerate((stacked, swapped)):
            high = half.astype(BF16)
            right[m, r * base:(r + 1) * base, :128] = high
            right[m, (2 + r) * base:(3 + r) * base, :128] = high
            right[m, r * base:(r + 1) * base, 128:] = (half - high.astype(F32)).astype(BF16)

    step_modes = min(256, modes // 2)
    step_blocks = step_modes // 8

    pieces = modes // 2 // step_modes

    def project(parity, to, m, i):
        both = dot(beam_t[m, parity, i * step_modes:(i + 1) * step_modes, :], right[m])
        sums = both[:, :128] + both[:, 128:]
        part[to, m, i * step_blocks:(i + 1) * step_blocks] = sums.reshape(step_blocks, 8, 128)

    to_core = []
    for m in range(mwin):
        for i in range(pieces):
            project(1 - core, 0, m, i)
            at = pl.ds(i * step_blocks, step_blocks)
            to_core.append(pltpu.make_async_remote_copy(
                part.at[0, m, at], core_recv.at[m, at], core_s.at[m, i], core_r.at[m, i],
                device_id={"chan": chan, "pair": chip * 2 + 1 - core}, device_id_type=MESH))
            to_core[-1].start()
    for m in range(mwin):
        for i in range(pieces):
            project(core, 1, m, i)

    top = jnp.zeros((8, 128), F32)
    step_chips = min(8, step_blocks)
    for m in range(mwin):
        for i in range(pieces):
            to_core[m * pieces + i].wait_recv()

            def merge(j, top, m=m, i=i):
                at = pl.ds(i * step_blocks + j * step_chips, step_chips)
                sums = part[1, m, at] + core_recv[m, at]
                part[1, m, at] = sums
                return jnp.maximum(top, jnp.max(jnp.abs(sums), axis=0))

            top = lax.fori_loop(0, step_blocks // step_chips, merge, top)
    peak = jnp.max(jnp.max(top, axis=1, keepdims=True), axis=0, keepdims=True)
    peak = jnp.maximum(peak, 1e-30)
    scale_send[...] = jnp.broadcast_to(peak * (1.0 / 32000.0), (1, 128))
    factor = jnp.broadcast_to(32000.0 / peak, (8, 128))

    def code_sums(i, carry):
        at = pl.ds(i * step_chips, step_chips)
        scaled = jnp.concatenate([part[1, 0, at] * factor, part[1, 1, at] * factor], axis=2)
        send2[at] = jnp.round(scaled).astype(I32).astype(I16)
        return carry

    lax.fori_loop(0, chips // step_chips, code_sums, 0)

    own_scale = pltpu.make_async_copy(scale_send, scale_recv.at[chip], scale_r)
    own_scale.start()
    own_red = pltpu.make_async_copy(send2.at[chip], recv2.at[chip], red_r)
    own_red.start()

    def send_red(peer):
        target = {"chan": chan, "pair": peer * 2 + core}
        pltpu.make_async_remote_copy(
            send2.at[peer], recv2.at[chip], red_s, red_r, device_id=target, device_id_type=MESH).start()
        pltpu.make_async_remote_copy(
            scale_send, scale_recv.at[chip], scale_s, scale_r, device_id=target, device_id_type=MESH).start()

    own_row(send_red)
    first_of = [lax.rem(chip_row + far(k, depth), depth) * side for k in range(depth)]
    spots = [lax.rem(chip_spot + far(k, side), side) for k in range(side)]
    for total in range(depth + side - 2):
        for k in range(max(0, total - side + 1), min(depth - 1, total + 1)):
            send_red(first_of[k] + spots[total - k])

    pltpu.make_async_copy(scale_recv, scale_recv, scale_r).wait()
    pltpu.make_async_copy(recv2, recv2, red_r).wait()

    step_adds = min(8, chips)

    def add_up(i, sums):
        for j in range(step_adds):
            scale = scale_recv[i * step_adds + j]
            sums = sums + recv2[i * step_adds + j].astype(I32).astype(F32) * jnp.concatenate([scale, scale], axis=1)
        return sums

    total = lax.fori_loop(0, chips // step_adds, add_up, jnp.zeros((8, columns), F32))
    total_buf[...] = total
    modes_out = pltpu.make_async_copy(total_buf, result_hbm, out_sem)
    modes_out.start()
    square = total * total
    power_0 = jnp.sum(square[:, :128], axis=1, keepdims=True)
    power_1 = jnp.sum(square[:, 128:], axis=1, keepdims=True)
    pow_send[...] = jnp.where(iota((8, 128), 1) == 0, power_0, power_1)
    own_power = pltpu.make_async_copy(pow_send, power_hbm.at[chan], own_sem)
    own_power.start()
    sends = []
    for i in range(1, nchan):
        peer = lax.rem(chan + i, nchan)
        copy = pltpu.make_async_remote_copy(
            pow_send, power_hbm.at[chan], pow_s.at[i], pow_r.at[i],
            device_id={"chan": peer, "pair": me}, device_id_type=MESH)
        copy.start()
        sends.append(copy)
    for copy in sends:
        copy.wait()
    own_power.wait()
    modes_out.wait()

    for copy in to_core:
        copy.wait_send()
    sent = 2 * groups

    @pl.when(keeper)
    def _():
        pltpu.make_async_copy(meta_send.at[pl.ds(0, sent - 1)], meta_send.at[pl.ds(0, sent - 1)], meta_s).wait()
        for i in range(1, nchan):
            pltpu.make_async_copy(meta_recv, meta_recv, hand_s.at[i]).wait()

    @pl.when(jnp.logical_not(keeper))
    def _():
        pltpu.make_async_copy(meta_send.at[pl.ds(0, sent)], meta_send.at[pl.ds(0, sent)], meta_s).wait()

    pltpu.make_async_copy(send.at[pl.ds(1, n - 1)], send.at[pl.ds(1, n - 1)], data_s).wait()
    pltpu.make_async_copy(send2.at[pl.ds(1, chips - 1)], send2.at[pl.ds(1, chips - 1)], red_s).wait()
    pltpu.make_async_copy(scale_recv.at[pl.ds(1, chips - 1)], scale_recv.at[pl.ds(1, chips - 1)], scale_s).wait()


def shape_results(mwin, sets, result_ref, powers_ref, modes_ref, power_ref):
    for m in range(mwin):
        for part in range(2):
            at = (2 * m + part) * sets
            modes_ref[:, m, part, :] = result_ref[:, at:at + sets]
    power = jnp.sum(powers_ref[...], axis=0) * (1.0 / (powers_ref.shape[0] * sets))
    power_ref[...] = jnp.transpose(power)[:mwin]


def per_device(visibility, pair_counts, owner_ids, slot_ids, beam):
    n, nchan = lax.axis_size("pair"), lax.axis_size("chan")
    rows, columns = visibility.shape[1:]
    mwin, _, base, modes = beam.shape[1:]
    sets = columns // (2 * mwin)
    chips = n // 2
    vmem, hbm = pl.BlockSpec(memory_space=pltpu.VMEM), pl.BlockSpec(memory_space=pltpu.HBM)
    dma = pltpu.SemaphoreType.DMA
    amplitudes, powers = pl.pallas_call(
        functools.partial(body, n, nchan, sets),
        out_shape=(
            jax.ShapeDtypeStruct((8, columns), F32),
            jax.ShapeDtypeStruct((nchan, 8, 128), F32),
        ),
        in_specs=[hbm] * 5,
        out_specs=(hbm, hbm),
        scratch_shapes=[
            pltpu.VMEM((1, rows), I32),
            pltpu.VMEM((1, rows), I32),
            pltpu.VMEM((1, rows), I32),
            pltpu.VMEM((rows, columns), BF16),
            pltpu.VMEM((n, 3, 8, 128), BF16),
            pltpu.VMEM((n, 3, 8, 128), BF16),
            pltpu.VMEM((n, 1, 128), F32),
            pltpu.VMEM((n, 1, 128), F32),
            pltpu.VMEM((mwin, 2, base, modes), F32),
            pltpu.VMEM((mwin, 2, modes // 2, 4 * base), BF16),
            pltpu.VMEM((base, n * 8), BF16),
            pltpu.VMEM((2 * base, n * 8), BF16),
            pltpu.VMEM((base, 128), F32),
            pltpu.VMEM((mwin, 4 * base, 256), BF16),
            pltpu.VMEM((2, mwin, chips, 8, 128), F32),
            pltpu.VMEM((mwin, chips, 8, 128), F32),
            pltpu.VMEM((chips, 8, columns), I16),
            pltpu.VMEM((chips, 8, columns), I16),
            pltpu.VMEM((1, 128), F32),
            pltpu.VMEM((chips, 1, 128), F32),
            pltpu.VMEM((8, columns), F32),
            pltpu.VMEM((8, 128), F32),
            dma((4,)), dma, dma, dma, dma((nchan,)), dma, dma, dma, dma((mwin, 2)), dma((mwin, 2)), dma, dma, dma, dma,
            dma((nchan,)), dma((nchan,)), dma, dma,
        ],
        compiler_params=pltpu.CompilerParams(
            collective_id=0, has_side_effects=True
        ),
        name="stack_project",
    )(
        owner_ids.reshape(1, rows), slot_ids.reshape(1, rows), pair_counts.reshape(1, rows),
        visibility[0], beam[0],
    )
    shaped, power = pl.pallas_call(
        functools.partial(shape_results, mwin, sets),
        out_shape=(jax.ShapeDtypeStruct((8, mwin, 2, sets), F32), jax.ShapeDtypeStruct((mwin, 8), F32)),
        in_specs=[vmem] * 2,
        out_specs=(vmem, vmem),
        name="shape_results",
    )(amplitudes, powers)
    return shaped[None], power.T


def solution(mesh):
    in_specs = (
        P("chan", "pair", None),
        P("pair"),
        P("pair", None),
        P("pair"),
        P("chan", None, None, "pair", None),
    )
    out_specs = (P("chan", "pair", None, None, None), P("pair", None))
    return jax.shard_map(
        per_device, mesh=mesh, in_specs=in_specs, out_specs=out_specs, check_vma=False
    )
```
